512 devices in a mesh: row: 16 (over x, y), col: 32 (over z, core).
Axes of the slice: x: 4, y: 4, z: 16, core: 2. Of those that a mesh axis runs over, the one named last changes fastest.
Arguments:
- hidden_states: bfloat16 [2048, 5120], P('row', 'col'), may hold values from -6 to 6
- clip_lengths: int32 [16, 2], P('row'), may hold values from 1 to 64, as said below
- modulation: bfloat16 [32, 3, 5120], P('row', None, 'col'), may hold values from -4 to 4
- fc1_weight: bfloat16 [5120, 13824], P('row', 'col'), may hold values from -0.078125 to 0.078125
- fc2_weight: bfloat16 [13824, 5120], P('col', 'row'), may hold values from -0.0546875 to 0.0546875
- out_grad: bfloat16 [2048, 5120], P('row', 'col'), may hold values from -6 to 6
Outputs:
- block_out: bfloat16 [2048, 5120], P('row', 'col')
- input_grad: bfloat16 [2048, 5120], P('row', 'col')
- modulation_grad: float32 [32, 3, 5120], P('row', None, 'col')
The draws below stay inside these ranges and needn't reach their ends.
Inputs may be any that keep to these rules, and one draw needn't show every extreme that they name: `clip_lengths`: in every draw the clip windows of some grid row all have 64 tokens.
All inputs are finite; a program needn't handle non-finite values.
Results may differ from the reference program's by a relative error of at most 0.0055.
Values may be sent and summed in bfloat16 or wider, within the bound.
A program may use at most 64 MiB of HBM per device.

```python
import jax
import jax.numpy as jnp
from jax import lax

D = 5120
FF = 13824
TOK_ROW = 128
CLIPS_ROW = 2
MOST = 64
GRID_ROWS = 16
TOKENS = 2048
CLIPS = 32


def draw_clip_lengths(key, part):
    counts = jax.random.randint(key, (GRID_ROWS, CLIPS_ROW), 1, MOST + 1)
    full_row = jax.random.randint(jax.random.fold_in(key, 7), (), 0, GRID_ROWS)
    chosen = jnp.arange(GRID_ROWS, dtype=jnp.int32)[:, None] == full_row
    return jnp.where(chosen, MOST, counts).astype(jnp.int32)


def shard_levels(stream_key, dims, cuts, least, high):
    factor_of = 1.0
    for position, blocks in cuts:
        draws = jax.random.uniform(jax.random.fold_in(jax.random.fold_in(stream_key, 6), position), (blocks,), jnp.float32, least / len(cuts), high / len(cuts))
        factor_of = factor_of * jnp.repeat(jnp.exp(draws), dims[position] // blocks).reshape((-1,) + (1,) * (len(dims) - 1 - position))
    return factor_of


def scatter_about(own_key, shape, scale, most, cuts=(), kind=jnp.bfloat16):
    entries = jax.random.normal(own_key, shape, jnp.float32) * scale
    if len(cuts) > 0:
        entries = shard_levels(own_key, shape, cuts, -0.22, 0.18) * entries
    return jnp.clip(entries, min=-most, max=most).astype(kind)


def setup_inputs(seed: int = 0) -> dict:
    splits = jax.random.split(jax.random.key(seed), 7)
    hidden_states = scatter_about(splits[0], (TOKENS, D), 1.0, 6.0, ((0, 16), (1, 32)))
    clip_lengths = draw_clip_lengths(jax.random.fold_in(splits[6], 71), 0)
    modulation = scatter_about(splits[2], (CLIPS, 3, D), 0.8, 4.0, ((0, 16), (2, 32)))
    fc1_weight = scatter_about(splits[3], (D, FF), D ** -0.5, 0.078125, ((0, 16), (1, 32)))
    fc2_weight = scatter_about(splits[4], (FF, D), FF ** -0.5, 0.0546875, ((0, 32), (1, 16)))
    out_grad = scatter_about(splits[5], (TOKENS, D), 1.0, 6.0, ((0, 16), (1, 32)))
    return dict(hidden_states=hidden_states, clip_lengths=clip_lengths, modulation=modulation, fc1_weight=fc1_weight, fc2_weight=fc2_weight, out_grad=out_grad)


epsilon = 1e-06

def gelu_slope(value):
    coeff = 0.7978845608028654
    inner = coeff * (value + 0.044715 * value * value * value)
    tangent = jnp.tanh(inner)
    return 0.5 * (1.0 + tangent) + 0.5 * value * (1.0 - tangent * tangent) * coeff * (1.0 + 3.0 * 0.044715 * value * value)

def reference(hidden_states, clip_lengths, modulation, fc1_weight, fc2_weight, out_grad):
    clip_ends = jnp.cumsum(clip_lengths, axis=1).astype(jnp.int32)
    places = jnp.arange(TOK_ROW, dtype=jnp.int32)
    segment = lax.optimization_barrier(jnp.sum((places[None, :, None] >= clip_ends[:, None, :]).astype(jnp.int32), axis=2))
    onehot = (segment[:, :, None] == jnp.arange(CLIPS_ROW, dtype=jnp.int32)[None, None, :]).astype(jnp.float32)
    live_rows = (segment < CLIPS_ROW).astype(jnp.float32).reshape(TOKENS, 1)
    mod_rows = modulation.astype(jnp.float32).reshape(GRID_ROWS, CLIPS_ROW, 3 * D)
    token_mod = jnp.einsum('gtc,gcd->gtd', onehot, mod_rows).reshape(TOKENS, 3, D)
    shift_tok = token_mod[:, 0]
    scale_tok = token_mod[:, 1]
    gate_tok = token_mod[:, 2]
    x_float = hidden_states.astype(jnp.float32)
    centre = lax.optimization_barrier(jnp.mean(x_float, axis=1, keepdims=True))
    deviation = x_float - centre
    inverse = lax.rsqrt(lax.optimization_barrier(jnp.mean(deviation * deviation, axis=1, keepdims=True)) + epsilon)
    normed = deviation * inverse
    modulated = (normed * (1.0 + scale_tok) + shift_tok).astype(jnp.bfloat16)
    pre_act = jnp.dot(modulated, fc1_weight, preferred_element_type=jnp.float32)
    activated = jax.nn.gelu(pre_act, approximate=True).astype(jnp.bfloat16)
    projected = jnp.dot(activated, fc2_weight, preferred_element_type=jnp.float32)
    block_out = (live_rows * (x_float + gate_tok * projected)).astype(jnp.bfloat16)
    grad_float = out_grad.astype(jnp.float32)
    z_grad = (live_rows * gate_tok * grad_float).astype(jnp.bfloat16)
    act_grad = lax.dot_general(z_grad, fc2_weight, (((1,), (1,)), ((), ())), preferred_element_type=jnp.float32)
    pre_grad = (act_grad * gelu_slope(pre_act)).astype(jnp.bfloat16)
    mod_in_grad = lax.dot_general(pre_grad, fc1_weight, (((1,), (1,)), ((), ())), preferred_element_type=jnp.float32)
    norm_grad = mod_in_grad * (1.0 + scale_tok)
    first_mean = lax.optimization_barrier(jnp.mean(norm_grad, axis=1, keepdims=True))
    second_mean = lax.optimization_barrier(jnp.mean(norm_grad * normed, axis=1, keepdims=True))
    input_grad = (live_rows * (grad_float + inverse * (norm_grad - first_mean - normed * second_mean))).astype(jnp.bfloat16)
    shift_grad = jnp.einsum('gtc,gtd->gcd', onehot, mod_in_grad.reshape(GRID_ROWS, TOK_ROW, D))
    scale_grad = jnp.einsum('gtc,gtd->gcd', onehot, (mod_in_grad * normed).reshape(GRID_ROWS, TOK_ROW, D))
    gate_grad = jnp.einsum('gtc,gtd->gcd', onehot, (projected * grad_float).reshape(GRID_ROWS, TOK_ROW, D))
    modulation_grad = jnp.stack([shift_grad, scale_grad, gate_grad], axis=2).reshape(CLIPS, 3, D)
    return (block_out, input_grad, modulation_grad)
```

```python
import jax
import jax.numpy as jnp
from jax import lax
from jax.experimental import pallas as pl
from jax.experimental.pallas import tpu as pltpu
from jax.sharding import PartitionSpec as P

EPSILON = 1e-06
COEFF = 0.7978845608028654
CUBIC = 0.044715
MESH = pl.DeviceIdType.MESH
F32 = jnp.float32
BF16 = jnp.bfloat16
SUM_TYPE = jnp.bfloat16

TOK = 128
FEAT = 160
HID = 432
ROWF = 320
MAIN = 256
REM = ROWF - MAIN
WIDE = MAIN + 2 * REM
QUARTERS = ((0, 112), (112, 112), (224, 112), (336, 96))
HALVES = ((0, 224), (224, 208))
MSG = FEAT + 16
SUMS = 16


def dot(a, b):
    return jnp.dot(a, b, preferred_element_type=F32)


def dot_tn(a, b):
    return lax.dot_general(a, b, (((0,), (0,)), ((), ())), preferred_element_type=F32)


def kernel(
    depth,
    side,
    w1_in,
    w2_in,
    msg_in,
    zg_in,
    pick_in,
    local_in,
    masks_in,
    block_out,
    input_out,
    mod_out,
    w1,
    w2,
    xg,
    zr,
    xm,
    pre,
    actg,
    act_t,
    pg_t,
    part_a,
    hand_a,
    part_b,
    hand_b,
    left_a,
    left_b,
    right_a,
    right_b,
    outl_a,
    outl_b,
    outr_a,
    outr_b,
    own_sem,
    w_send,
    w_recv,
    z_send,
    z_recv,
    p_send,
    p_recv,
    h_send,
    h_recv,
    s_send,
    s_recv,
):
    n_dev = depth
    row = lax.axis_index("row")
    col = lax.axis_index("col")
    px, py = row // side, row % side
    z, core = col // 2, col % 2

    def wrap(value, size):
        return lax.rem(value + 2 * size, size)

    def row_of(dx, dy):
        return wrap(px + dx, side) * side + wrap(py + dy, side)

    def col_of(dz):
        return wrap(z + dz, n_dev) * 2 + core

    def at_row(dx, dy):
        return (row_of(dx, dy), col)

    def at_col(dz):
        return (row, col_of(dz))

    partner = (row, z * 2 + (1 - core))
    neighbours = [
        at_row(1, 0),
        at_row(-1, 0),
        at_row(0, 1),
        at_row(0, -1),
        at_col(1),
        at_col(-1),
        partner,
    ]

    own = [
        pltpu.make_async_copy(w1_in, w1.at[row], own_sem.at[0]),
        pltpu.make_async_copy(msg_in, xg.at[z, core], own_sem.at[1]),
        pltpu.make_async_copy(
            zg_in, zr.at[z, pl.ds(pl.multiple_of(core * FEAT, FEAT), FEAT)], own_sem.at[2]
        ),
        pltpu.make_async_copy(w2_in, w2.at[row], own_sem.at[3]),
    ]
    for copy in own:
        copy.start()

    barrier = pltpu.get_barrier_semaphore()
    for device in neighbours:
        pl.semaphore_signal(barrier, inc=1, device_id=device, device_id_type=MESH)

    def clear(k, carry):
        zr[k, ROWF:, :] = jnp.zeros((REM, TOK), BF16)
        xm[k, MAIN:ROWF, :] = jnp.zeros((REM, 2 * TOK), BF16)
        return carry

    lax.fori_loop(0, n_dev, clear, 0)
    pl.semaphore_wait(barrier, len(neighbours))

    pending = []

    def send(ref, at, device, ssem, rsem):
        copy = pltpu.make_async_remote_copy(
            src_ref=ref.at[at],
            dst_ref=ref.at[at],
            send_sem=ssem,
            recv_sem=rsem,
            device_id=device,
            device_id_type=MESH,
        )
        copy.start()
        pending.append(copy)

    def arrive(ref, at, device, ssem, rsem):
        pltpu.make_async_remote_copy(
            src_ref=ref.at[at],
            dst_ref=ref.at[at],
            send_sem=ssem,
            recv_sem=rsem,
            device_id=device,
            device_id_type=MESH,
        ).wait_recv()

    class Ring:
        def __init__(self, weight, half, group, base, along):
            self.ref = (w1, w2)[weight]
            self.weight, self.half, self.group = weight, half, group
            self.base, self.along = base, along

        def slot(self, offset):
            dx, dy = self.base
            if self.along == 0:
                return row_of(dx + offset, dy)
            return row_of(dx, dy + offset)

        def peer(self, offset):
            return at_row(offset, 0) if self.along == 0 else at_row(0, offset)

        def sems(self, i):
            at = (self.weight, self.half, self.group, i)
            return w_send.at[at], w_recv.at[at]

        def rows(self, quarter):
            if quarter is None:
                return pl.ds(*HALVES[self.half])
            return pl.ds(*QUARTERS[2 * self.half + quarter])

        def move(self, fn, offset, quarter, to, i):
            fn(self.ref, (self.slot(offset), self.rows(quarter)), self.peer(to), *self.sems(i))

        def start(self):
            self.move(send, 0, None, 1, 0)
            self.move(send, 0, None, -1, 1)

        def middle(self, side_of):
            if side_of < 0:
                self.move(arrive, -1, None, -1, 0)
                self.move(send, -1, 0, 1, 2)
            else:
                self.move(arrive, 1, None, 1, 1)
                self.move(send, 1, 1, -1, 3)

        def end(self):
            self.move(arrive, 2, 0, -1, 2)
            self.move(arrive, 2, 1, 1, 3)

    def rings_of(weight):
        first, second = [], []
        for half in (0, 1):
            first.append(Ring(weight, half, 0, (0, 0), half))
            for i, offset in enumerate((0, -1, 1, 2)):
                base = (offset, 0) if half == 0 else (0, offset)
                second.append(Ring(weight, half, 1 + i, base, 1 - half))
        return first, second

    def weight_steps(weight):
        first, second = rings_of(weight)

        def begin():
            for ring in first:
                ring.start()
            second[0].start()
            second[4].start()

        def near():
            for half in (0, 1):
                first[half].middle(-1)
                second[4 * half + 1].start()
            for half in (0, 1):
                first[half].middle(1)
                second[4 * half + 2].start()

        def far():
            for half in (0, 1):
                first[half].end()
                second[4 * half + 3].start()

        def pass_on(i):
            def act():
                for half in (0, 1):
                    second[4 * half + i].middle(-1)
                    second[4 * half + i].middle(1)

            return act

        def finish(i):
            def act():
                for half in (0, 1):
                    second[4 * half + i].end()

            return act

        return begin, near, far, [pass_on(i) for i in range(4)], [finish(i) for i in range(4)]

    begin1, near1, far1, pass1, end1 = weight_steps(0)
    begin2, near2, far2, pass2, end2 = weight_steps(1)

    def message(m, dz, who):
        k = wrap(z + dz, n_dev)
        if m == 0:
            return xg, (k, who)
        return zr, (k, pl.ds(pl.multiple_of(who * FEAT, FEAT), FEAT))

    def hand_over(m, dz, i):
        ref, at = message(m, dz, core)
        send(ref, at, partner, p_send.at[m, i], p_recv.at[m, i])

    half_z = n_dev // 2

    def z_begin():
        for m in (0, 1):
            ref, at = message(m, 0, core)
            send(ref, at, at_col(1), z_send.at[m, 0, 0], z_recv.at[m, 0, 0])
            send(ref, at, at_col(-1), z_send.at[m, 1, 0], z_recv.at[m, 1, 0])
            hand_over(m, 0, 0)

    def z_step(s):
        def act():
            for m in (0, 1):
                ref, at = message(m, -s, core)
                arrive(ref, at, at_col(-1), z_send.at[m, 0, s - 1], z_recv.at[m, 0, s - 1])
                if s < half_z:
                    send(ref, at, at_col(1), z_send.at[m, 0, s], z_recv.at[m, 0, s])
                hand_over(m, -s, 2 * s - 1)
                if s < half_z:
                    ref, at = message(m, s, core)
                    arrive(ref, at, at_col(1), z_send.at[m, 1, s - 1], z_recv.at[m, 1, s - 1])
                    if s < half_z - 1:
                        send(ref, at, at_col(-1), z_send.at[m, 1, s], z_recv.at[m, 1, s])
                    hand_over(m, s, 2 * s)

        return act

    def z_handed(m):
        def take(dz, i):
            ref, at = message(m, dz, 1 - core)
            arrive(ref, at, partner, p_send.at[m, i], p_recv.at[m, i])

        def act():
            take(0, 0)
            for s in range(1, half_z + 1):
                take(-s, 2 * s - 1)
                if s < half_z:
                    take(s, 2 * s)

        return act

    own[0].wait()
    begin1()
    own[1].wait()
    own[2].wait()
    z_begin()
    own[3].wait()
    z_step(1)()
    near1()
    z_step(2)()
    z_step(3)()
    far1()
    begin2()
    pass1[0]()
    z_step(4)()
    pass1[1]()
    z_step(5)()
    pass1[2]()
    z_step(6)()
    near2()
    pass1[3]()
    z_step(7)()
    z_step(8)()
    z_handed(0)()

    def add_up(k, carry):
        x = xg[k, :, :FEAT, :].astype(F32)
        return carry + jnp.sum(x.reshape(2 * FEAT, TOK), axis=0, keepdims=True)

    width = n_dev * 2 * FEAT
    centre = lax.fori_loop(0, n_dev, add_up, jnp.zeros((1, TOK), F32)) / width

    def add_square(k, carry):
        x = xg[k, :, :FEAT, :].astype(F32).reshape(2 * FEAT, TOK) - centre
        return carry + jnp.sum(x * x, axis=0, keepdims=True)

    spread = lax.fori_loop(0, n_dev, add_square, jnp.zeros((1, TOK), F32)) / width
    inverse = lax.rsqrt(spread + EPSILON)

    far2()
    pick = pick_in[...]

    def modulate(k, carry):
        for j in (0, 1):
            x = (xg[k, j, :FEAT, :].astype(F32) - centre) * inverse
            wide = dot_tn(xg[k, j, FEAT:, :], pick)
            top = (x[:TOK] * (1.0 + wide[:, :TOK]) + wide[:, TOK : 2 * TOK]).astype(BF16)
            low = wide[: FEAT - TOK]
            rest = (x[TOK:] * (1.0 + low[:, 2 * TOK : 3 * TOK]) + low[:, 3 * TOK : 4 * TOK]).astype(
                BF16
            )
            top_mod = wide[:, 4 * TOK : 5 * TOK].astype(BF16)
            rest_mod = low[:, 5 * TOK :].astype(BF16)
            if j == 0:
                xm[k, 0:128, 0:TOK] = top
                xm[k, 128:160, 0:TOK] = rest
                xm[k, 0:128, TOK:] = top_mod
                xm[k, 128:160, TOK:] = rest_mod
            else:
                xm[k, 160:256, 0:TOK] = top[:96]
                xm[k, 320:352, 0:TOK] = top[96:]
                xm[k, 352:384, 0:TOK] = rest
                xm[k, 160:256, TOK:] = top_mod[:96]
                xm[k, 320:352, TOK:] = top_mod[96:]
                xm[k, 352:384, TOK:] = rest_mod
        return carry

    lax.fori_loop(0, n_dev, modulate, 0)

    pass2[0]()
    for act in end1:
        act()
    pass2[1]()
    z_handed(1)()

    pre[...] = jnp.zeros((HID, 2 * TOK), F32)

    def first(k, carry):
        pre[...] += dot(w1[k], xm[k])
        return carry

    lax.fori_loop(0, n_dev // 2, first, 0)
    pass2[2]()
    lax.fori_loop(n_dev // 2, n_dev, first, 0)

    def tangent_of(v):
        return jnp.tanh(COEFF * (v + CUBIC * v * v * v))

    def split_store(ref, value):
        for start in range(0, HID, TOK):
            stop = min(start + TOK, HID)
            ref[:, start:stop] = value[start:stop].T.astype(BF16)

    v = pre[:, :TOK]
    split_store(act_t, 0.5 * v * (1.0 + tangent_of(v)))
    pass2[3]()
    for act in end2:
        act()

    class Sum:
        def __init__(self, i, part, hand, left, right, outl, outr):
            self.i = i
            self.part, self.hand = part, hand
            self.left, self.right, self.outl, self.outr = left, right, outl, outr

        def owner(self, way, s):
            if way == 0:
                return wrap(z - half_z - 1 + s, n_dev)
            if way == 1:
                return wrap(z + half_z - s, n_dev)
            return z

        def hand_over(self, way, s):
            d = self.owner(way, s)
            i = (s - 1, half_z + s - 1, 2 * half_z - 1)[way]
            copy = pltpu.make_async_remote_copy(
                src_ref=self.part.at[d, 1 - core],
                dst_ref=self.hand.at[d],
                send_sem=h_send.at[self.i, i],
                recv_sem=h_recv.at[self.i, i],
                device_id=partner,
                device_id_type=MESH,
            )
            copy.start()
            pending.append(copy)

        def both_cores(self, way, s):
            d = self.owner(way, s)
            i = (s - 1, half_z + s - 1, 2 * half_z - 1)[way]
            arrive(self.hand, d, partner, h_send.at[self.i, i], h_recv.at[self.i, i])
            return self.part[d, core] + self.hand[d]

        def from_chain(self, way, s):
            ref = (self.left, self.right)[way]
            at = (self.i, way, s)
            arrive(ref, s, at_col((1, -1)[way]), s_send.at[at], s_recv.at[at])
            return ref[s].astype(F32)

        def step(self, s):
            for way in (0, 1):
                if way == 1 and s == half_z:
                    continue
                total = self.both_cores(way, s)
                if s > 1:
                    total = total + self.from_chain(way, s - 2)
                out = (self.outl, self.outr)[way]
                land = (self.left, self.right)[way]
                out[s - 1] = total.astype(SUM_TYPE)
                at = (self.i, way, s - 1)
                copy = pltpu.make_async_remote_copy(
                    src_ref=out.at[s - 1],
                    dst_ref=land.at[s - 1],
                    send_sem=s_send.at[at],
                    recv_sem=s_recv.at[at],
                    device_id=at_col((-1, 1)[way]),
                    device_id_type=MESH,
                )
                copy.start()
                pending.append(copy)

        def last(self):
            total = self.both_cores(2, 1)
            total = total + self.from_chain(0, half_z - 1)
            return total + self.from_chain(1, half_z - 2)

    sum_a = Sum(0, part_a, hand_a, left_a, right_a, outl_a, outr_a)
    sum_b = Sum(1, part_b, hand_b, left_b, right_b, outl_b, outr_b)

    def forward_block(way, s):
        d = sum_a.owner(way, s)
        acted = act_t[...]
        main = dot(acted, w2[d]).T
        rest = dot(acted, w1[d, :, MAIN:]).T
        part_a[d, 0] = main[:FEAT]
        part_a[d, 1, : MAIN - FEAT] = main[FEAT:]
        part_a[d, 1, MAIN - FEAT :] = rest[:REM]
        sum_a.hand_over(way, s)

    def backward_block(way, s):
        d = sum_b.owner(way, s)
        both = dot(pg_t[...], w1[d])
        main = both[:, :MAIN].T
        rest = both[:, MAIN:].T
        part_b[d, 0, :FEAT] = main[:FEAT]
        part_b[d, 1, : MAIN - FEAT] = main[FEAT:]
        part_b[d, 1, MAIN - FEAT : FEAT] = rest[REM:]
        sum_b.hand_over(way, s)

    def blocks(fn, s):
        if s > half_z:
            return
        fn(0, s)
        fn(1, s) if s < half_z else fn(2, 1)

    for s in range(1, 4):
        blocks(forward_block, s)
    sum_a.step(1)

    actg[...] = jnp.zeros((HID, TOK), F32)

    def second(k, carry):
        actg[...] += dot(w2[k], zr[k, :MAIN]) + dot(w1[k, :, MAIN:], zr[k, MAIN:])
        return carry

    lax.fori_loop(0, n_dev, second, 0)
    v = pre[:, :TOK]
    tangent = tangent_of(v)
    slope = 0.5 * (1.0 + tangent) + 0.5 * v * (1.0 - tangent * tangent) * COEFF * (
        1.0 + 3.0 * CUBIC * v * v
    )
    grad = (actg[...] * slope).astype(BF16).astype(F32)
    split_store(pg_t, grad)

    in_first = masks_in[0:1, :] > 0.0
    extra = pre[:, TOK:]
    ones = extra[:, 4:5]
    scaled = ones + jnp.where(in_first, extra[:, 0:1], extra[:, 1:2])
    shifted = jnp.where(in_first, extra[:, 2:3], extra[:, 3:4])
    sums = jnp.concatenate(
        [
            jnp.sum(grad * scaled, axis=0, keepdims=True),
            jnp.sum(grad * (v - shifted), axis=0, keepdims=True),
            jnp.zeros((SUMS - 2, TOK), F32),
        ],
        axis=0,
    )

    def put_sums(k, carry):
        part_b[k, 0, FEAT:] = sums
        part_b[k, 1, FEAT:] = sums
        return carry

    lax.fori_loop(0, n_dev, put_sums, 0)

    blocks(backward_block, 1)
    blocks(backward_block, 2)
    for s in range(1, half_z + 1):
        if s > 1:
            sum_a.step(s)
        sum_b.step(s)
        blocks(backward_block, s + 2)
        blocks(forward_block, s + 3)

    first_mask = masks_in[0:1, :]
    second_mask = masks_in[1:2, :]
    live = masks_in[2:3, :]
    x = xg[z, core, :FEAT, :].astype(F32)
    normed = (x - centre) * inverse
    gate = local_in[0]
    scale_one = 1.0 + local_in[1]
    g = local_in[2]
    lane = lax.broadcasted_iota(jnp.int32, (FEAT, TOK), 1)

    def put(lanes, index, value):
        a = jnp.sum(value * first_mask, axis=1, keepdims=True)
        b = jnp.sum(value * second_mask, axis=1, keepdims=True)
        lanes = jnp.where(lane == index, a, lanes)
        return jnp.where(lane == index + 3, b, lanes)

    projected = sum_a.last()
    block_out[...] = (live * (x + gate * projected)).astype(BF16)
    lanes = put(jnp.zeros((FEAT, TOK), F32), 2, projected * g)

    total = sum_b.last()
    mod_in = total[:FEAT]
    first_mean = total[FEAT : FEAT + 1] / width
    second_mean = total[FEAT + 1 : FEAT + 2] / width
    norm_grad = mod_in * scale_one
    input_out[...] = (
        live * (g + inverse * (norm_grad - first_mean - normed * second_mean))
    ).astype(BF16)
    lanes = put(lanes, 0, mod_in)
    mod_out[...] = put(lanes, 1, mod_in * normed)

    for copy in pending:
        copy.wait_send()


def body(hidden_states, clip_lengths, modulation, fc1_weight, fc2_weight, out_grad):
    depth = lax.axis_size("col") // 2
    side = 4
    clip_ends = jnp.cumsum(clip_lengths[0])
    places = jnp.arange(TOK, dtype=jnp.int32)
    segment = jnp.sum((places[None, :] >= clip_ends[:, None]).astype(jnp.int32), axis=0)
    is_clip = (segment[None, :] == jnp.arange(2, dtype=jnp.int32)[:, None]).astype(F32)
    live = (segment < 2).astype(F32)[None, :]
    masks = jnp.concatenate([is_clip, live, jnp.zeros((5, TOK), F32)], axis=0)
    mod_t = modulation.astype(F32).transpose(1, 2, 0)
    per_token = mod_t[:, :, 0:1] * is_clip[0][None, None] + mod_t[:, :, 1:2] * is_clip[1][None, None]
    g = out_grad.T.astype(F32)
    local = jnp.stack([per_token[2], per_token[1], g])
    zg = (live * per_token[2] * g).astype(BF16)

    rows = jnp.concatenate(
        [modulation[:, 1], modulation[:, 0], jnp.ones((1, FEAT), BF16), jnp.zeros((3, FEAT), BF16)],
        axis=0,
    )
    low = jnp.pad(rows[:, TOK:], ((0, 0), (0, 2 * TOK - FEAT)))
    msg = jnp.concatenate([hidden_states.T, rows[:, :TOK], low], axis=0)

    onehot = is_clip.astype(BF16)
    zero2 = jnp.zeros((2, TOK), BF16)
    zero4 = jnp.zeros((4, TOK), BF16)
    scale_rows = jnp.concatenate([onehot, zero2, zero4], axis=0)
    shift_rows = jnp.concatenate([zero2, onehot, zero4], axis=0)
    eye = jnp.eye(8, TOK, dtype=BF16)
    zero8 = jnp.zeros((8, TOK), BF16)
    pick = jnp.concatenate(
        [
            jnp.concatenate([scale_rows, shift_rows, zero8, zero8, eye, zero8], axis=1),
            jnp.concatenate([zero8, zero8, scale_rows, shift_rows, zero8, eye], axis=1),
        ],
        axis=0,
    )
    w1_t = fc1_weight.T
    w1_in = jnp.concatenate([w1_t[:, :MAIN], fc2_weight[:, MAIN:], w1_t[:, MAIN:]], axis=1)
    w2_in = fc2_weight[:, :MAIN]

    vmem = pl.BlockSpec(memory_space=pltpu.VMEM)
    anywhere = pl.BlockSpec(memory_space=pl.ANY)
    dma = pltpu.SemaphoreType.DMA
    half_z = depth // 2
    block, grad, mods = pl.pallas_call(
        lambda *refs: kernel(depth, side, *refs),
        out_shape=(
            jax.ShapeDtypeStruct((FEAT, TOK), BF16),
            jax.ShapeDtypeStruct((FEAT, TOK), BF16),
            jax.ShapeDtypeStruct((FEAT, TOK), F32),
        ),
        in_specs=[anywhere] * 4 + [vmem] * 3,
        out_specs=(vmem, vmem, vmem),
        scratch_shapes=[
            pltpu.VMEM((16, HID, WIDE), BF16),
            pltpu.VMEM((16, HID, MAIN), BF16),
            pltpu.VMEM((depth, 2, MSG, TOK), BF16),
            pltpu.VMEM((depth, WIDE, TOK), BF16),
            pltpu.VMEM((depth, WIDE, 2 * TOK), BF16),
            pltpu.VMEM((HID, 2 * TOK), F32),
            pltpu.VMEM((HID, TOK), F32),
            pltpu.VMEM((TOK, HID), BF16),
            pltpu.VMEM((TOK, HID), BF16),
            pltpu.VMEM((depth, 2, FEAT, TOK), F32),
            pltpu.VMEM((depth, FEAT, TOK), F32),
            pltpu.VMEM((depth, 2, FEAT + SUMS, TOK), F32),
            pltpu.VMEM((depth, FEAT + SUMS, TOK), F32),
            pltpu.VMEM((half_z, FEAT, TOK), SUM_TYPE),
            pltpu.VMEM((half_z, FEAT + SUMS, TOK), SUM_TYPE),
            pltpu.VMEM((half_z, FEAT, TOK), SUM_TYPE),
            pltpu.VMEM((half_z, FEAT + SUMS, TOK), SUM_TYPE),
            pltpu.VMEM((half_z, FEAT, TOK), SUM_TYPE),
            pltpu.VMEM((half_z, FEAT + SUMS, TOK), SUM_TYPE),
            pltpu.VMEM((half_z, FEAT, TOK), SUM_TYPE),
            pltpu.VMEM((half_z, FEAT + SUMS, TOK), SUM_TYPE),
            dma((4,)),
            dma((2, 2, 5, 4)),
            dma((2, 2, 5, 4)),
            dma((2, 2, half_z)),
            dma((2, 2, half_z)),
            dma((2, depth)),
            dma((2, depth)),
            dma((2, depth)),
            dma((2, depth)),
            dma((2, 2, half_z)),
            dma((2, 2, half_z)),
        ],
        compiler_params=pltpu.CompilerParams(
            collective_id=0, has_side_effects=True, vmem_limit_bytes=60000 * 1024
        ),
    )(w1_in, w2_in, msg, zg, pick, local, masks)
    modulation_grad = mods[:, :6].T.reshape(2, 3, FEAT)
    return block.T, grad.T, modulation_grad


def solution(mesh):
    return jax.shard_map(
        body,
        mesh=mesh,
        in_specs=(
            P("row", "col"),
            P("row", None),
            P("row", None, "col"),
            P("row", "col"),
            P("col", "row"),
            P("row", "col"),
        ),
        out_specs=(P("row", "col"), P("row", "col"), P("row", None, "col")),
        check_vma=False,
    )
```

```python
import jax
import jax.numpy as jnp
from jax import lax
from jax.experimental import pallas as pl
from jax.experimental.pallas import tpu as pltpu
from jax.sharding import PartitionSpec as P

EPSILON = 1e-06
COEFF = 0.7978845608028654
CUBIC = 0.044715
MESH = pl.DeviceIdType.MESH
F32 = jnp.float32
BF16 = jnp.bfloat16
SUM_TYPE = jnp.bfloat16

TOK = 128
FEAT = 160
HID = 432
ROWF = 320
MAIN = 256
REM = ROWF - MAIN
WIDE = MAIN + 2 * REM
QUARTERS = ((0, 112), (112, 112), (224, 112), (336, 96))
HALVES = ((0, 224), (224, 208))
MSG = FEAT + 16
SUMS = 16


def dot(a, b):
    return jnp.dot(a, b, preferred_element_type=F32)


def dot_tn(a, b):
    return lax.dot_general(a, b, (((0,), (0,)), ((), ())), preferred_element_type=F32)


def kernel(
    depth,
    side,
    hidden_in,
    lengths_in,
    mod_in,
    fc1_in,
    fc2_in,
    grad_in,
    block_out,
    input_out,
    mod_out,
    w1,
    w2,
    xg,
    zr,
    xm,
    pre,
    actg,
    act_t,
    pg_t,
    part_a,
    hand_a,
    part_b,
    hand_b,
    near_in_a,
    near_in_b,
    near_out_a,
    near_out_b,
    far_in_a,
    far_in_b,
    far_out_a,
    far_out_b,
    local,
    w_send,
    w_recv,
    z_send,
    z_recv,
    p_send,
    p_recv,
    h_send,
    h_recv,
    s_send,
    s_recv,
):
    n_dev = depth
    row = lax.axis_index("row")
    col = lax.axis_index("col")
    px, py = row // side, row % side
    z, core = col // 2, col % 2

    def wrap(value, size):
        return lax.rem(value + 2 * size, size)

    def row_of(dx, dy):
        return wrap(px + dx, side) * side + wrap(py + dy, side)

    def col_of(dz):
        return wrap(z + dz, n_dev) * 2 + core

    def at_row(dx, dy):
        return (row_of(dx, dy), col)

    def at_col(dz):
        return (row, col_of(dz))

    partner = (row, z * 2 + (1 - core))
    neighbours = [
        at_row(1, 0),
        at_row(-1, 0),
        at_row(0, 1),
        at_row(0, -1),
        partner,
    ] + [at_col(step) for step in (1, -1, 2, -2, 4, -4, 8)]

    barrier = pltpu.get_barrier_semaphore()
    for device in neighbours:
        pl.semaphore_signal(barrier, inc=1, device_id=device, device_id_type=MESH)

    def clear(k, carry):
        zr[k, ROWF:, :] = jnp.zeros((REM, TOK), BF16)
        xm[k, MAIN:ROWF, :] = jnp.zeros((REM, 2 * TOK), BF16)
        return carry

    def flip(value):
        return value.astype(F32).T

    def own_weights(start, size):
        at = pl.ds(start, size)
        for f in range(0, MAIN, TOK):
            w1[row, at, f : f + TOK] = flip(fc1_in[f : f + TOK, at]).astype(BF16)
        both = jnp.concatenate([flip(fc2_in[at, MAIN:]), fc1_in[MAIN:, at].astype(F32)], axis=0)
        w1[row, at, MAIN:] = both.T.astype(BF16)

    for start in range(0, HID, TOK):
        own_weights(start, min(TOK, HID - start))
    w2[row] = fc2_in[:, :MAIN]
    pl.semaphore_wait(barrier, len(neighbours))

    pending = []

    def send(ref, at, device, ssem, rsem):
        copy = pltpu.make_async_remote_copy(
            src_ref=ref.at[at],
            dst_ref=ref.at[at],
            send_sem=ssem,
            recv_sem=rsem,
            device_id=device,
            device_id_type=MESH,
        )
        copy.start()
        pending.append(copy)

    def arrive(ref, at, device, ssem, rsem):
        pltpu.make_async_remote_copy(
            src_ref=ref.at[at],
            dst_ref=ref.at[at],
            send_sem=ssem,
            recv_sem=rsem,
            device_id=device,
            device_id_type=MESH,
        ).wait_recv()

    class Ring:
        def __init__(self, weight, half, group, base, along):
            self.ref = (w1, w2)[weight]
            self.weight, self.half, self.group = weight, half, group
            self.base, self.along = base, along

        def slot(self, offset):
            dx, dy = self.base
            if self.along == 0:
                return row_of(dx + offset, dy)
            return row_of(dx, dy + offset)

        def peer(self, offset):
            return at_row(offset, 0) if self.along == 0 else at_row(0, offset)

        def sems(self, i):
            at = (self.weight, self.half, self.group, i)
            return w_send.at[at], w_recv.at[at]

        def rows(self, quarter):
            if quarter is None:
                return pl.ds(*HALVES[self.half])
            return pl.ds(*QUARTERS[2 * self.half + quarter])

        def move(self, fn, offset, quarter, to, i):
            fn(self.ref, (self.slot(offset), self.rows(quarter)), self.peer(to), *self.sems(i))

        def start(self):
            self.move(send, 0, None, 1, 0)
            self.move(send, 0, None, -1, 1)

        def middle(self, side_of):
            if side_of < 0:
                self.move(arrive, -1, None, -1, 0)
                self.move(send, -1, 0, 1, 2)
            else:
                self.move(arrive, 1, None, 1, 1)
                self.move(send, 1, 1, -1, 3)

        def end(self):
            self.move(arrive, 2, 0, -1, 2)
            self.move(arrive, 2, 1, 1, 3)

    def rings_of(weight):
        first, second = [], []
        for half in (0, 1):
            first.append(Ring(weight, half, 0, (0, 0), half))
            for i, offset in enumerate((0, -1, 1, 2)):
                base = (offset, 0) if half == 0 else (0, offset)
                second.append(Ring(weight, half, 1 + i, base, 1 - half))
        return first, second

    def weight_steps(weight):
        first, second = rings_of(weight)

        def begin():
            for ring in first:
                ring.start()
            second[0].start()
            second[4].start()

        def near():
            for half in (0, 1):
                first[half].middle(-1)
                second[4 * half + 1].start()
            for half in (0, 1):
                first[half].middle(1)
                second[4 * half + 2].start()

        def far():
            for half in (0, 1):
                first[half].end()
                second[4 * half + 3].start()

        def pass_on(i):
            def act():
                for half in (0, 1):
                    second[4 * half + i].middle(-1)
                    second[4 * half + i].middle(1)

            return act

        def finish(i):
            def act():
                for half in (0, 1):
                    second[4 * half + i].end()

            return act

        return begin, near, far, [pass_on(i) for i in range(4)], [finish(i) for i in range(4)]

    begin1, near1, far1, pass1, end1 = weight_steps(0)
    begin2, near2, far2, pass2, end2 = weight_steps(1)

    def message(m, dz, who):
        k = wrap(z + dz, n_dev)
        if m == 0:
            return xg, (k, who)
        return zr, (k, pl.ds(pl.multiple_of(who * FEAT, FEAT), FEAT))

    def hand_over(m, dz, i):
        ref, at = message(m, dz, core)
        send(ref, at, partner, p_send.at[m, i], p_recv.at[m, i])

    jumps = (8, 4, -4)
    near_by = (1, -1, 2)

    def base(j):
        return 0 if j == 0 else -jumps[j - 1]

    def spread(m, j):
        ref, at = message(m, base(j), core)
        for i, step in enumerate(near_by):
            n = 3 + 3 * j + i
            send(ref, at, at_col(step), z_send.at[m, n], z_recv.at[m, n])

    def z_begin(m):
        ref, at = message(m, 0, core)
        for i, jump in enumerate(jumps):
            send(ref, at, at_col(jump), z_send.at[m, i], z_recv.at[m, i])
        spread(m, 0)
        hand_over(m, 0, 0)

    def z_jump(m):
        for i, jump in enumerate(jumps):
            ref, at = message(m, -jump, core)
            arrive(ref, at, at_col(-jump), z_send.at[m, i], z_recv.at[m, i])
            spread(m, i + 1)
            hand_over(m, -jump, i + 1)

    def z_near(m, j):
        for i, step in enumerate(near_by):
            n = 3 + 3 * j + i
            ref, at = message(m, base(j) - step, core)
            arrive(ref, at, at_col(-step), z_send.at[m, n], z_recv.at[m, n])
            hand_over(m, base(j) - step, 4 + 3 * j + i)

    def z_handed(m):
        for j in range(4):
            for i in range(4):
                offset = base(j) - ((0,) + near_by)[i]
                n = j if i == 0 else 3 + 3 * j + i
                ref, at = message(m, offset, 1 - core)
                arrive(ref, at, partner, p_send.at[m, n], p_recv.at[m, n])

    begin1()

    lane = lax.broadcasted_iota(jnp.int32, (1, TOK), 1)
    end_one = lengths_in[0, 0]
    end_two = end_one + lengths_in[0, 1]
    ones_row = jnp.ones((1, TOK), F32)
    zero_row = jnp.zeros((1, TOK), F32)
    in_one = lane < end_one
    first_mask = jnp.where(in_one, ones_row, zero_row)
    live = jnp.where(lane < end_two, ones_row, zero_row)
    second_mask = live - first_mask

    def flip_tokens(ref):
        return jnp.concatenate([flip(ref[:, :TOK]), flip(ref[:, TOK:])], axis=0)

    xg[z, core, :FEAT, :] = flip_tokens(hidden_in).astype(BF16)
    mods_one, mods_two = mod_in[0].astype(F32), mod_in[1].astype(F32)
    at_row8 = lax.broadcasted_iota(jnp.int32, (8, FEAT), 0)
    rows = jnp.where(at_row8 == 4, 1.0, jnp.zeros((8, FEAT), F32))
    for i, source in enumerate((1, 0)):
        rows = jnp.where(at_row8 == 2 * i, mods_one[source : source + 1], rows)
        rows = jnp.where(at_row8 == 2 * i + 1, mods_two[source : source + 1], rows)
    rows = jnp.where(at_row8 == 5, mods_one[2:3], rows)
    rows = jnp.where(at_row8 == 6, mods_two[2:3], rows)
    tail = lax.broadcasted_iota(jnp.int32, (FEAT, TOK), 0) - TOK
    shift_lanes = jnp.where(
        tail == lax.broadcasted_iota(jnp.int32, (FEAT, TOK), 1),
        jnp.ones((FEAT, TOK), F32),
        jnp.zeros((FEAT, TOK), F32),
    ).astype(BF16)
    tile = jnp.concatenate([rows[:, :TOK], dot(rows.astype(BF16), shift_lanes)], axis=0).astype(BF16)
    xg[z, core, FEAT:, :] = tile

    pick_row = lax.broadcasted_iota(jnp.int32, (16, TOK), 0)
    pick_lane = lax.broadcasted_iota(jnp.int32, (16, TOK), 1)
    pick_zero = jnp.zeros((16, TOK), F32)

    def picker(at):
        low = jnp.where(pick_row == at + 1, second_mask, pick_zero)
        return jnp.where(pick_row == at, first_mask, low)

    def lanes_of(base):
        inside = (pick_row - base == pick_lane) & (pick_lane < 8)
        return jnp.where(inside, 1.0, pick_zero)

    pick = jnp.concatenate(
        [picker(0), picker(2), picker(8), picker(10), lanes_of(0), lanes_of(8)], axis=1
    ).astype(BF16)
    pick_gate = jnp.concatenate([picker(5), picker(13)], axis=1).astype(BF16)
    gates = dot_tn(tile, pick_gate)
    gate_here = jnp.concatenate([gates[:, :TOK], gates[: FEAT - TOK, TOK:]], axis=0)
    g_here = flip_tokens(grad_in)
    local[0] = gate_here
    local[1] = g_here
    zr[z, pl.ds(pl.multiple_of(core * FEAT, FEAT), FEAT), :] = (live * gate_here * g_here).astype(
        BF16
    )
    z_begin(0)
    z_begin(1)
    lax.fori_loop(0, n_dev, clear, 0)
    near1()
    z_jump(0)
    far1()
    begin2()
    pass1[0]()
    z_jump(1)
    z_near(0, 0)
    pass1[1]()
    z_near(0, 1)
    z_near(0, 2)
    pass1[2]()
    z_near(0, 3)
    pass1[3]()
    z_handed(0)
    near2()

    def add_up(k, carry):
        x = xg[k, :, :FEAT, :].astype(F32)
        return carry + jnp.sum(x.reshape(2 * FEAT, TOK), axis=0, keepdims=True)

    width = n_dev * 2 * FEAT
    centre = lax.fori_loop(0, n_dev, add_up, jnp.zeros((1, TOK), F32)) / width

    def add_square(k, carry):
        x = xg[k, :, :FEAT, :].astype(F32).reshape(2 * FEAT, TOK) - centre
        return carry + jnp.sum(x * x, axis=0, keepdims=True)

    spread = lax.fori_loop(0, n_dev, add_square, jnp.zeros((1, TOK), F32)) / width
    inverse = lax.rsqrt(spread + EPSILON)

    far2()
    def modulate(k, carry):
        for j in (0, 1):
            x = (xg[k, j, :FEAT, :].astype(F32) - centre) * inverse
            wide = dot_tn(xg[k, j, FEAT:, :], pick)
            top = (x[:TOK] * (1.0 + wide[:, :TOK]) + wide[:, TOK : 2 * TOK]).astype(BF16)
            low = wide[: FEAT - TOK]
            rest = (x[TOK:] * (1.0 + low[:, 2 * TOK : 3 * TOK]) + low[:, 3 * TOK : 4 * TOK]).astype(
                BF16
            )
            top_mod = wide[:, 4 * TOK : 5 * TOK].astype(BF16)
            rest_mod = low[:, 5 * TOK :].astype(BF16)
            if j == 0:
                xm[k, 0:128, 0:TOK] = top
                xm[k, 128:160, 0:TOK] = rest
                xm[k, 0:128, TOK:] = top_mod
                xm[k, 128:160, TOK:] = rest_mod
            else:
                xm[k, 160:256, 0:TOK] = top[:96]
                xm[k, 320:352, 0:TOK] = top[96:]
                xm[k, 352:384, 0:TOK] = rest
                xm[k, 160:256, TOK:] = top_mod[:96]
                xm[k, 320:352, TOK:] = top_mod[96:]
                xm[k, 352:384, TOK:] = rest_mod
        return carry

    lax.fori_loop(0, n_dev // 2, modulate, 0)
    z_near(1, 0)
    z_near(1, 1)
    pass2[0]()
    lax.fori_loop(n_dev // 2, n_dev, modulate, 0)
    z_near(1, 2)
    z_near(1, 3)
    pass2[1]()
    for act in end1:
        act()

    pre[...] = jnp.zeros((HID, 2 * TOK), F32)

    def first(k, carry):
        pre[...] += dot(w1[k], xm[k])
        return carry

    lax.fori_loop(0, n_dev // 2, first, 0)
    pass2[2]()
    lax.fori_loop(n_dev // 2, n_dev, first, 0)
    pass2[3]()
    z_handed(1)

    def tangent_of(v):
        return jnp.tanh(COEFF * (v + CUBIC * v * v * v))

    def split_store(ref, value):
        for start in range(0, HID, TOK):
            stop = min(start + TOK, HID)
            ref[:, start:stop] = value[start:stop].T.astype(BF16)

    v = pre[:, :TOK]
    split_store(act_t, 0.5 * v * (1.0 + tangent_of(v)))

    class Sum:
        def __init__(self, i, part, hand, near_in, near_out, far_in, far_out):
            self.i = i
            self.part, self.hand = part, hand
            self.near_in, self.near_out = near_in, near_out
            self.far_in, self.far_out = far_in, far_out

        def both_cores(self, d):
            return self.part[d, core] + self.hand[d]

        def hand_over(self, d):
            copy = pltpu.make_async_remote_copy(
                src_ref=self.part.at[d, 1 - core],
                dst_ref=self.hand.at[d],
                send_sem=h_send.at[self.i, d],
                recv_sem=h_recv.at[self.i, d],
                device_id=partner,
                device_id_type=MESH,
            )
            copy.start()
            pending.append(copy)

        def near_copy(self, slot, far):
            n = 4 * slot + far
            return pltpu.make_async_remote_copy(
                src_ref=self.near_out.at[slot, far],
                dst_ref=self.near_in.at[slot, far],
                send_sem=s_send.at[self.i, n],
                recv_sem=s_recv.at[self.i, n],
                device_id=at_col(slot - 1),
                device_id_type=MESH,
            )

        def near(self, d):
            place = wrap(d - z, n_dev) + 1
            slot, far = lax.rem(place, 4), lax.rem(place // 4, 4)
            arrive(self.hand, d, partner, h_send.at[self.i, d], h_recv.at[self.i, d])

            @pl.when(slot != 1)
            def _():
                self.near_out[slot, far] = self.both_cores(d).astype(SUM_TYPE)
                self.near_copy(slot, far).start()

        def gathered(self, far):
            total = self.both_cores(wrap(z + 4 * far, n_dev))
            for slot in (0, 2, 3):
                self.near_copy(slot, far).wait_recv()
                total = total + self.near_in[slot, far].astype(F32)
            return total

        def far_copy(self, far):
            return pltpu.make_async_remote_copy(
                src_ref=self.far_out.at[far],
                dst_ref=self.far_in.at[far],
                send_sem=s_send.at[self.i, 16 + far],
                recv_sem=s_recv.at[self.i, 16 + far],
                device_id=at_col(4 * far),
                device_id_type=MESH,
            )

        def far(self, far):
            self.far_out[far] = self.gathered(far).astype(SUM_TYPE)
            self.far_copy(far).start()

        def last(self):
            total = self.gathered(0)
            for far in (1, 3, 2):
                self.far_copy(far).wait_recv()
                total = total + self.far_in[far].astype(F32)
            return total

        def sent(self):
            for far in range(4):
                for slot in (0, 2, 3):
                    self.near_copy(slot, far).wait_send()
                if far > 0:
                    self.far_copy(far).wait_send()

    sum_a = Sum(0, part_a, hand_a, near_in_a, near_out_a, far_in_a, far_out_a)
    sum_b = Sum(1, part_b, hand_b, near_in_b, near_out_b, far_in_b, far_out_b)

    def forward_block(d):
        acted = act_t[...]
        main = dot(acted, w2[d]).T
        rest = dot(acted, w1[d, :, MAIN:]).T
        part_a[d, 0] = main[:FEAT]
        part_a[d, 1, : MAIN - FEAT] = main[FEAT:]
        part_a[d, 1, MAIN - FEAT :] = rest[:REM]
        sum_a.hand_over(d)

    def backward_block(d):
        both = dot(pg_t[...], w1[d])
        main = both[:, :MAIN].T
        rest = both[:, MAIN:].T
        part_b[d, 0, :FEAT] = main[:FEAT]
        part_b[d, 1, : MAIN - FEAT] = main[FEAT:]
        part_b[d, 1, MAIN - FEAT : FEAT] = rest[REM:]
        sum_b.hand_over(d)

    actg[...] = jnp.zeros((HID, TOK), F32)
    offsets = (0, -1, 1, 2)

    def second(group):
        for half in (0, 1):
            rows = pl.ds(*HALVES[half])

            def step(t, carry):
                k = row_of(offsets[group], t) if half == 0 else row_of(t, offsets[group])
                actg[rows] += dot(w2[k, rows], zr[k, :MAIN]) + dot(
                    w1[k, rows, MAIN:], zr[k, MAIN:]
                )
                return carry

            lax.fori_loop(0, side, step, 0)

    def whole(group):
        return [
            row_of(offsets[a], offsets[b])
            for a in range(group + 1)
            for b in range(group + 1)
            if max(a, b) == group
        ]

    waiting = []
    for group in range(4):
        end2[group]()
        second(group)
        if group < 3:
            for d in whole(group):
                forward_block(d)
            for d in waiting:
                sum_a.near(d)
            waiting = whole(group)

    v = pre[:, :TOK]
    tangent = tangent_of(v)
    slope = 0.5 * (1.0 + tangent) + 0.5 * v * (1.0 - tangent * tangent) * COEFF * (
        1.0 + 3.0 * CUBIC * v * v
    )
    grad = (actg[...] * slope).astype(BF16).astype(F32)
    split_store(pg_t, grad)

    extra = pre[:, TOK:]
    ones = extra[:, 4:5]
    scaled = ones + jnp.where(in_one, extra[:, 0:1], extra[:, 1:2])
    shifted = jnp.where(in_one, extra[:, 2:3], extra[:, 3:4])
    sums = jnp.concatenate(
        [
            jnp.sum(grad * scaled, axis=0, keepdims=True),
            jnp.sum(grad * (v - shifted), axis=0, keepdims=True),
            jnp.zeros((SUMS - 2, TOK), F32),
        ],
        axis=0,
    )

    def put_sums(k, carry):
        part_b[k, 0, FEAT:] = sums
        part_b[k, 1, FEAT:] = sums
        return carry

    lax.fori_loop(0, n_dev, put_sums, 0)

    def batch(far):
        return [wrap(z + slot - 1 + 4 * far, n_dev) for slot in (3, 2, 0, 1)]

    def backward(far):
        for d in batch(far):
            backward_block(d)
        for d in batch(far):
            sum_b.near(d)

    backward(2)
    for d in waiting:
        sum_a.near(d)
    backward(1)
    for d in whole(3):
        forward_block(d)
    sum_b.far(2)
    backward(3)
    for d in whole(3):
        sum_a.near(d)
    sum_b.far(1)
    backward(0)
    sum_b.far(3)
    for far in (2, 1, 3):
        sum_a.far(far)

    x = xg[z, core, :FEAT, :].astype(F32)
    normed = (x - centre) * inverse
    gate = local[0]
    g = local[1]
    mine = dot_tn(tile, pick[:, : 4 * TOK])
    scale_one = 1.0 + jnp.concatenate(
        [mine[:, :TOK], mine[: FEAT - TOK, 2 * TOK : 3 * TOK]], axis=0
    )
    lane_at = lax.broadcasted_iota(jnp.int32, (FEAT, TOK), 1)

    def put(lanes, index, value):
        a = jnp.sum(value * first_mask, axis=1, keepdims=True)
        b = jnp.sum(value * second_mask, axis=1, keepdims=True)
        lanes = jnp.where(lane_at == index, a, lanes)
        return jnp.where(lane_at == index + 8, b, lanes)

    projected = sum_a.last()
    out = live * (x + gate * projected)
    block_out[:, :TOK] = out[:TOK].T.astype(BF16)
    block_out[:, TOK:] = out[TOK:].T.astype(BF16)
    lanes = put(jnp.zeros((FEAT, TOK), F32), 2, projected * g)

    total = sum_b.last()
    mod_grad = total[:FEAT]
    first_mean = total[FEAT : FEAT + 1] / width
    second_mean = total[FEAT + 1 : FEAT + 2] / width
    norm_grad = mod_grad * scale_one
    out = live * (g + inverse * (norm_grad - first_mean - normed * second_mean))
    input_out[:, :TOK] = out[:TOK].T.astype(BF16)
    input_out[:, TOK:] = out[TOK:].T.astype(BF16)
    lanes = put(lanes, 0, mod_grad)
    lanes = put(lanes, 1, mod_grad * normed)
    high, low = lanes[:TOK].T, lanes[TOK:].T
    for clip in (0, 1):
        mod_out[clip, :, :TOK] = high[8 * clip : 8 * clip + 3]
        mod_out[clip, :, TOK:] = low[8 * clip : 8 * clip + 3]

    sum_a.sent()
    sum_b.sent()
    for copy in pending:
        copy.wait_send()


def body(hidden_states, clip_lengths, modulation, fc1_weight, fc2_weight, out_grad):
    depth = lax.axis_size("col") // 2
    side = 4
    vmem = pl.BlockSpec(memory_space=pltpu.VMEM)
    smem = pl.BlockSpec(memory_space=pltpu.SMEM)
    dma = pltpu.SemaphoreType.DMA
    return pl.pallas_call(
        lambda *refs: kernel(depth, side, *refs),
        out_shape=(
            jax.ShapeDtypeStruct((TOK, FEAT), BF16),
            jax.ShapeDtypeStruct((TOK, FEAT), BF16),
            jax.ShapeDtypeStruct((2, 3, FEAT), F32),
        ),
        in_specs=[vmem, smem] + [vmem] * 4,
        out_specs=(vmem, vmem, vmem),
        scratch_shapes=[
            pltpu.VMEM((16, HID, WIDE), BF16),
            pltpu.VMEM((16, HID, MAIN), BF16),
            pltpu.VMEM((depth, 2, MSG, TOK), BF16),
            pltpu.VMEM((depth, WIDE, TOK), BF16),
            pltpu.VMEM((depth, WIDE, 2 * TOK), BF16),
            pltpu.VMEM((HID, 2 * TOK), F32),
            pltpu.VMEM((HID, TOK), F32),
            pltpu.VMEM((TOK, HID), BF16),
            pltpu.VMEM((TOK, HID), BF16),
            pltpu.VMEM((depth, 2, FEAT, TOK), F32),
            pltpu.VMEM((depth, FEAT, TOK), F32),
            pltpu.VMEM((depth, 2, FEAT + SUMS, TOK), F32),
            pltpu.VMEM((depth, FEAT + SUMS, TOK), F32),
            pltpu.VMEM((4, 4, FEAT, TOK), SUM_TYPE),
            pltpu.VMEM((4, 4, FEAT + SUMS, TOK), SUM_TYPE),
            pltpu.VMEM((4, 4, FEAT, TOK), SUM_TYPE),
            pltpu.VMEM((4, 4, FEAT + SUMS, TOK), SUM_TYPE),
            pltpu.VMEM((4, FEAT, TOK), SUM_TYPE),
            pltpu.VMEM((4, FEAT + SUMS, TOK), SUM_TYPE),
            pltpu.VMEM((4, FEAT, TOK), SUM_TYPE),
            pltpu.VMEM((4, FEAT + SUMS, TOK), SUM_TYPE),
            pltpu.VMEM((2, FEAT, TOK), F32),
            dma((2, 2, 5, 4)),
            dma((2, 2, 5, 4)),
            dma((2, 15)),
            dma((2, 15)),
            dma((2, depth)),
            dma((2, depth)),
            dma((2, depth)),
            dma((2, depth)),
            dma((2, 20)),
            dma((2, 20)),
        ],
        compiler_params=pltpu.CompilerParams(
            collective_id=0, has_side_effects=True, vmem_limit_bytes=60000 * 1024
        ),
    )(hidden_states, clip_lengths, modulation, fc1_weight, fc2_weight, out_grad)


def solution(mesh):
    return jax.shard_map(
        body,
        mesh=mesh,
        in_specs=(
            P("row", "col"),
            P("row", None),
            P("row", None, "col"),
            P("row", "col"),
            P("col", "row"),
            P("row", "col"),
        ),
        out_specs=(P("row", "col"), P("row", "col"), P("row", None, "col")),
        check_vma=False,
    )
```

```python
import jax
import jax.numpy as jnp
from jax import lax
from jax.experimental import pallas as pl
from jax.experimental.pallas import tpu as pltpu
from jax.sharding import PartitionSpec as P

EPSILON = 1e-06
COEFF = 0.7978845608028654
CUBIC = 0.044715
MESH = pl.DeviceIdType.MESH
F32 = jnp.float32
BF16 = jnp.bfloat16
SUM_TYPE = jnp.bfloat16

TOK = 128
FEAT = 160
HID = 432
ROWF = 320
MAIN = 256
REM = ROWF - MAIN
WIDE = MAIN + 2 * REM
QUARTERS = ((0, 112), (112, 112), (224, 112), (336, 96))
HALVES = ((0, 224), (224, 208))
MSG = FEAT + 16
SUMS = 16


def dot(a, b):
    return jnp.dot(a, b, preferred_element_type=F32)


def dot_tn(a, b):
    return lax.dot_general(a, b, (((0,), (0,)), ((), ())), preferred_element_type=F32)


def kernel(
    depth,
    side,
    hidden_in,
    lengths_in,
    mod_in,
    fc1_in,
    fc2_in,
    grad_in,
    block_out,
    input_out,
    mod_out,
    w1,
    w2,
    xg,
    zr,
    xm,
    pre,
    actg,
    act_t,
    pg_t,
    part_a,
    hand_a,
    part_b,
    hand_b,
    near_in_a,
    near_in_b,
    near_out_a,
    near_out_b,
    far_in_a,
    far_in_b,
    far_out_a,
    far_out_b,
    local,
    w_send,
    w_recv,
    z_send,
    z_recv,
    p_send,
    p_recv,
    h_send,
    h_recv,
    s_send,
    s_recv,
):
    n_dev = depth
    row = lax.axis_index("row")
    col = lax.axis_index("col")
    px, py = row // side, row % side
    z, core = col // 2, col % 2

    def wrap(value, size):
        return lax.rem(value + 2 * size, size)

    def row_of(dx, dy):
        return wrap(px + dx, side) * side + wrap(py + dy, side)

    def col_of(dz):
        return wrap(z + dz, n_dev) * 2 + core

    def at_row(dx, dy):
        return (row_of(dx, dy), col)

    way = 1 - 2 * core

    def at_col(dz):
        return (row, col_of(way * dz))

    partner = (row, z * 2 + (1 - core))
    neighbours = [
        at_row(1, 0),
        at_row(-1, 0),
        at_row(0, 1),
        at_row(0, -1),
        partner,
    ] + [at_col(step) for step in (1, -1, 2, -2, 4, -4)]

    barrier = pltpu.get_barrier_semaphore()
    for device in neighbours:
        pl.semaphore_signal(barrier, inc=1, device_id=device, device_id_type=MESH)

    def clear(k, carry):
        zr[k, ROWF:, :] = jnp.zeros((REM, TOK), BF16)
        xm[k, MAIN:ROWF, :] = jnp.zeros((REM, 2 * TOK), BF16)
        return carry

    def flip(value):
        return value.astype(F32).T

    def own_weights(start, size):
        at = pl.ds(start, size)
        for f in range(0, MAIN, TOK):
            w1[row, at, f : f + TOK] = flip(fc1_in[f : f + TOK, at]).astype(BF16)
            w2[row, at, f : f + TOK] = flip(fc2_in[f : f + TOK, at]).astype(BF16)
        both = jnp.concatenate([fc2_in[MAIN:, at], fc1_in[MAIN:, at]], axis=0)
        w1[row, at, MAIN:] = flip(both).astype(BF16)

    for start in range(0, HID, TOK):
        own_weights(start, min(TOK, HID - start))
    pl.semaphore_wait(barrier, len(neighbours))

    pending = []

    def send(ref, at, device, ssem, rsem):
        copy = pltpu.make_async_remote_copy(
            src_ref=ref.at[at],
            dst_ref=ref.at[at],
            send_sem=ssem,
            recv_sem=rsem,
            device_id=device,
            device_id_type=MESH,
        )
        copy.start()
        pending.append(copy)

    def arrive(ref, at, device, ssem, rsem):
        pltpu.make_async_remote_copy(
            src_ref=ref.at[at],
            dst_ref=ref.at[at],
            send_sem=ssem,
            recv_sem=rsem,
            device_id=device,
            device_id_type=MESH,
        ).wait_recv()

    class Ring:
        def __init__(self, weight, half, group, base, along):
            self.ref = (w1, w2)[weight]
            self.weight, self.half, self.group = weight, half, group
            self.base, self.along = base, along

        def slot(self, offset):
            dx, dy = self.base
            if self.along == 0:
                return row_of(dx + offset, dy)
            return row_of(dx, dy + offset)

        def peer(self, offset):
            return at_row(offset, 0) if self.along == 0 else at_row(0, offset)

        def sems(self, i):
            at = (self.weight, self.half, self.group, i)
            return w_send.at[at], w_recv.at[at]

        def rows(self, quarter):
            if quarter is None:
                return pl.ds(*HALVES[self.half])
            return pl.ds(*QUARTERS[2 * self.half + quarter])

        def move(self, fn, offset, quarter, to, i):
            fn(self.ref, (self.slot(offset), self.rows(quarter)), self.peer(to), *self.sems(i))

        def start(self):
            self.move(send, 0, None, 1, 0)
            self.move(send, 0, None, -1, 1)

        def middle(self, side_of):
            if side_of < 0:
                self.move(arrive, -1, None, -1, 0)
                self.move(send, -1, 0, 1, 2)
            else:
                self.move(arrive, 1, None, 1, 1)
                self.move(send, 1, 1, -1, 3)

        def end(self):
            self.move(arrive, 2, 0, -1, 2)
            self.move(arrive, 2, 1, 1, 3)

    def rings_of(weight):
        first, second = [], []
        for half in (0, 1):
            first.append(Ring(weight, half, 0, (0, 0), half))
            for i, offset in enumerate((0, -1, 1, 2)):
                base = (offset, 0) if half == 0 else (0, offset)
                second.append(Ring(weight, half, 1 + i, base, 1 - half))
        return first, second

    def weight_steps(weight):
        first, second = rings_of(weight)

        def begin():
            for ring in first:
                ring.start()
            second[0].start()
            second[4].start()

        def near():
            for half in (0, 1):
                first[half].middle(-1)
                second[4 * half + 1].start()
            for half in (0, 1):
                first[half].middle(1)
                second[4 * half + 2].start()

        def far():
            for half in (0, 1):
                first[half].end()
                second[4 * half + 3].start()

        def pass_on(i):
            def act():
                for half in (0, 1):
                    second[4 * half + i].middle(-1)
                    second[4 * half + i].middle(1)

            return act

        def finish(i):
            def act():
                for half in (0, 1):
                    second[4 * half + i].end()

            return act

        return begin, near, far, [pass_on(i) for i in range(4)], [finish(i) for i in range(4)]

    begin1, near1, far1, pass1, end1 = weight_steps(0)
    begin2, near2, far2, pass2, end2 = weight_steps(1)

    def message(m, dz, who):
        k = wrap(z + (way if who is core else -way) * dz, n_dev)
        if m == 0:
            return xg, (k, who)
        return zr, (k, pl.ds(pl.multiple_of(who * FEAT, FEAT), FEAT))

    def hand_over(m, dz, i):
        ref, at = message(m, dz, core)
        send(ref, at, partner, p_send.at[m, i], p_recv.at[m, i])

    near_by = (1, -1, 2)
    bases = (0, -4, 4, 8)

    def base(j):
        return bases[j]

    def spread(m, j):
        ref, at = message(m, base(j), core)
        for i, step in enumerate(near_by):
            n = 3 + 3 * j + i
            send(ref, at, at_col(step), z_send.at[m, n], z_recv.at[m, n])

    def z_begin(m):
        ref, at = message(m, 0, core)
        for n, step in ((0, 4), (1, -4)):
            send(ref, at, at_col(step), z_send.at[m, n], z_recv.at[m, n])
        spread(m, 0)
        hand_over(m, 0, 0)

    def z_jump(m):
        ref, at = message(m, -4, core)
        arrive(ref, at, at_col(-4), z_send.at[m, 0], z_recv.at[m, 0])
        send(ref, at, at_col(4), z_send.at[m, 2], z_recv.at[m, 2])
        spread(m, 1)
        hand_over(m, -4, 1)
        ref, at = message(m, 4, core)
        arrive(ref, at, at_col(4), z_send.at[m, 1], z_recv.at[m, 1])
        spread(m, 2)
        hand_over(m, 4, 2)

    def z_jump_far(m):
        ref, at = message(m, -8, core)
        arrive(ref, at, at_col(-4), z_send.at[m, 2], z_recv.at[m, 2])
        spread(m, 3)
        hand_over(m, 8, 3)

    def z_near(m, j):
        for i, step in enumerate(near_by):
            n = 3 + 3 * j + i
            ref, at = message(m, base(j) - step, core)
            arrive(ref, at, at_col(-step), z_send.at[m, n], z_recv.at[m, n])
            hand_over(m, base(j) - step, 4 + 3 * j + i)

    def z_handed(m):
        for j in range(4):
            for i in range(4):
                offset = base(j) - ((0,) + near_by)[i]
                n = j if i == 0 else 3 + 3 * j + i
                ref, at = message(m, offset, 1 - core)
                arrive(ref, at, partner, p_send.at[m, n], p_recv.at[m, n])

    begin1()

    lane = lax.broadcasted_iota(jnp.int32, (1, TOK), 1)
    end_one = lengths_in[0, 0]
    end_two = end_one + lengths_in[0, 1]
    ones_row = jnp.ones((1, TOK), F32)
    zero_row = jnp.zeros((1, TOK), F32)
    in_one = lane < end_one
    first_mask = jnp.where(in_one, ones_row, zero_row)
    live = jnp.where(lane < end_two, ones_row, zero_row)
    second_mask = live - first_mask

    xg[z, core, :FEAT, :] = hidden_in[...]
    mods = [mod_in[i].astype(F32) for i in range(3)]
    at_row8 = lax.broadcasted_iota(jnp.int32, (8, FEAT), 0)
    rows = jnp.where(at_row8 == 4, 1.0, jnp.zeros((8, FEAT), F32))
    for i, source in enumerate((1, 0)):
        rows = jnp.where(at_row8 == 2 * i, mods[source][0:1], rows)
        rows = jnp.where(at_row8 == 2 * i + 1, mods[source][1:2], rows)
    rows = jnp.where(at_row8 == 5, mods[2][0:1], rows)
    rows = jnp.where(at_row8 == 6, mods[2][1:2], rows)
    tail = lax.broadcasted_iota(jnp.int32, (FEAT, TOK), 0) - TOK
    shift_lanes = jnp.where(
        tail == lax.broadcasted_iota(jnp.int32, (FEAT, TOK), 1),
        jnp.ones((FEAT, TOK), F32),
        jnp.zeros((FEAT, TOK), F32),
    ).astype(BF16)
    tile = jnp.concatenate([rows[:, :TOK], dot(rows.astype(BF16), shift_lanes)], axis=0).astype(BF16)
    xg[z, core, FEAT:, :] = tile

    pick_row = lax.broadcasted_iota(jnp.int32, (16, TOK), 0)
    pick_lane = lax.broadcasted_iota(jnp.int32, (16, TOK), 1)
    pick_zero = jnp.zeros((16, TOK), F32)

    def picker(at):
        low = jnp.where(pick_row == at + 1, second_mask, pick_zero)
        return jnp.where(pick_row == at, first_mask, low)

    def lanes_of(base):
        inside = (pick_row - base == pick_lane) & (pick_lane < 8)
        return jnp.where(inside, 1.0, pick_zero)

    pick = jnp.concatenate(
        [picker(0), picker(2), picker(8), picker(10), lanes_of(0), lanes_of(8)], axis=1
    ).astype(BF16)
    pick_gate = jnp.concatenate([picker(5), picker(13)], axis=1).astype(BF16)
    gates = dot_tn(tile, pick_gate)
    gate_here = jnp.concatenate([gates[:, :TOK], gates[: FEAT - TOK, TOK:]], axis=0)
    g_here = grad_in[...].astype(F32)
    local[0] = gate_here
    local[1] = g_here
    zr[z, pl.ds(pl.multiple_of(core * FEAT, FEAT), FEAT), :] = (live * gate_here * g_here).astype(
        BF16
    )
    z_begin(0)
    z_begin(1)
    lax.fori_loop(0, n_dev, clear, 0)
    near1()
    z_jump(0)
    far1()
    begin2()
    pass1[0]()
    z_jump_far(0)
    z_jump(1)
    z_near(0, 0)
    pass1[1]()
    z_near(0, 1)
    z_near(0, 2)
    pass1[2]()
    z_jump_far(1)
    z_near(0, 3)
    pass1[3]()
    z_handed(0)
    near2()

    def add_up(k, carry):
        x = xg[k, :, :FEAT, :].astype(F32)
        return carry + jnp.sum(x.reshape(2 * FEAT, TOK), axis=0, keepdims=True)

    width = n_dev * 2 * FEAT
    centre = lax.fori_loop(0, n_dev, add_up, jnp.zeros((1, TOK), F32)) / width

    def add_square(k, carry):
        x = xg[k, :, :FEAT, :].astype(F32).reshape(2 * FEAT, TOK) - centre
        return carry + jnp.sum(x * x, axis=0, keepdims=True)

    spread = lax.fori_loop(0, n_dev, add_square, jnp.zeros((1, TOK), F32)) / width
    inverse = lax.rsqrt(spread + EPSILON)

    far2()
    def modulate(k, carry):
        for j in (0, 1):
            x = (xg[k, j, :FEAT, :].astype(F32) - centre) * inverse
            wide = dot_tn(xg[k, j, FEAT:, :], pick)
            top = (x[:TOK] * (1.0 + wide[:, :TOK]) + wide[:, TOK : 2 * TOK]).astype(BF16)
            low = wide[: FEAT - TOK]
            rest = (x[TOK:] * (1.0 + low[:, 2 * TOK : 3 * TOK]) + low[:, 3 * TOK : 4 * TOK]).astype(
                BF16
            )
            top_mod = wide[:, 4 * TOK : 5 * TOK].astype(BF16)
            rest_mod = low[:, 5 * TOK :].astype(BF16)
            if j == 0:
                xm[k, 0:128, 0:TOK] = top
                xm[k, 128:160, 0:TOK] = rest
                xm[k, 0:128, TOK:] = top_mod
                xm[k, 128:160, TOK:] = rest_mod
            else:
                xm[k, 160:256, 0:TOK] = top[:96]
                xm[k, 320:352, 0:TOK] = top[96:]
                xm[k, 352:384, 0:TOK] = rest
                xm[k, 160:256, TOK:] = top_mod[:96]
                xm[k, 320:352, TOK:] = top_mod[96:]
                xm[k, 352:384, TOK:] = rest_mod
        return carry

    lax.fori_loop(0, n_dev // 2, modulate, 0)
    z_near(1, 0)
    z_near(1, 1)
    pass2[0]()
    lax.fori_loop(n_dev // 2, n_dev, modulate, 0)
    z_near(1, 2)
    z_near(1, 3)
    pass2[1]()
    for act in end1:
        act()

    pre[...] = jnp.zeros((HID, 2 * TOK), F32)

    def first(k, carry):
        pre[...] += dot(w1[k], xm[k])
        return carry

    lax.fori_loop(0, n_dev // 2, first, 0)
    pass2[2]()
    lax.fori_loop(n_dev // 2, n_dev, first, 0)
    pass2[3]()
    z_handed(1)

    def tangent_of(v):
        return jnp.tanh(COEFF * (v + CUBIC * v * v * v))

    def split_store(ref, value):
        for start in range(0, HID, TOK):
            stop = min(start + TOK, HID)
            ref[:, start:stop] = value[start:stop].T.astype(BF16)

    v = pre[:, :TOK]
    split_store(act_t, 0.5 * v * (1.0 + tangent_of(v)))

    class Sum:
        def __init__(self, i, part, hand, near_in, near_out, far_in, far_out):
            self.i = i
            self.part, self.hand = part, hand
            self.near_in, self.near_out = near_in, near_out
            self.far_in, self.far_out = far_in, far_out

        def both_cores(self, d):
            return self.part[d, core] + self.hand[d]

        def hand_over(self, d):
            copy = pltpu.make_async_remote_copy(
                src_ref=self.part.at[d, 1 - core],
                dst_ref=self.hand.at[d],
                send_sem=h_send.at[self.i, d],
                recv_sem=h_recv.at[self.i, d],
                device_id=partner,
                device_id_type=MESH,
            )
            copy.start()
            pending.append(copy)

        def near_copy(self, slot, far):
            n = 4 * slot + far
            return pltpu.make_async_remote_copy(
                src_ref=self.near_out.at[slot, far],
                dst_ref=self.near_in.at[slot, far],
                send_sem=s_send.at[self.i, n],
                recv_sem=s_recv.at[self.i, n],
                device_id=at_col(slot - 1),
                device_id_type=MESH,
            )

        def near(self, d):
            place = wrap(way * (d - z), n_dev) + 1
            slot, far = lax.rem(place, 4), lax.rem(place // 4, 4)
            arrive(self.hand, d, partner, h_send.at[self.i, d], h_recv.at[self.i, d])

            @pl.when(slot != 1)
            def _():
                self.near_out[slot, far] = self.both_cores(d).astype(SUM_TYPE)
                self.near_copy(slot, far).start()

        def gathered(self, far):
            total = self.both_cores(wrap(z + way * 4 * far, n_dev))
            for slot in (0, 2, 3):
                self.near_copy(slot, far).wait_recv()
                total = total + self.near_in[slot, far].astype(F32)
            return total

        def far_copy(self, far):
            return pltpu.make_async_remote_copy(
                src_ref=self.far_out.at[far],
                dst_ref=self.far_in.at[far],
                send_sem=s_send.at[self.i, 16 + far],
                recv_sem=s_recv.at[self.i, 16 + far],
                device_id=at_col(-4 if far == 3 else 4),
                device_id_type=MESH,
            )

        def arrived(self, far):
            self.far_copy(far).wait_recv()
            return self.far_in[far].astype(F32)

        def far(self, far):
            total = self.gathered(far)
            if far == 1:
                total = total + self.arrived(2)
            self.far_out[far] = total.astype(SUM_TYPE)
            self.far_copy(far).start()

        def last(self):
            total = self.gathered(0)
            for far in (3, 1):
                total = total + self.arrived(far)
            return total

        def sent(self):
            for far in range(4):
                for slot in (0, 2, 3):
                    self.near_copy(slot, far).wait_send()
                if far > 0:
                    self.far_copy(far).wait_send()

    sum_a = Sum(0, part_a, hand_a, near_in_a, near_out_a, far_in_a, far_out_a)
    sum_b = Sum(1, part_b, hand_b, near_in_b, near_out_b, far_in_b, far_out_b)

    def forward_block(d):
        acted = act_t[...]
        main = dot(acted, w2[d]).T
        rest = dot(acted, w1[d, :, MAIN:]).T
        part_a[d, 0] = main[:FEAT]
        part_a[d, 1, : MAIN - FEAT] = main[FEAT:]
        part_a[d, 1, MAIN - FEAT :] = rest[:REM]
        sum_a.hand_over(d)

    def backward_block(d):
        both = dot(pg_t[...], w1[d])
        main = both[:, :MAIN].T
        rest = both[:, MAIN:].T
        part_b[d, 0, :FEAT] = main[:FEAT]
        part_b[d, 1, : MAIN - FEAT] = main[FEAT:]
        part_b[d, 1, MAIN - FEAT : FEAT] = rest[REM:]
        sum_b.hand_over(d)

    actg[...] = jnp.zeros((HID, TOK), F32)
    offsets = (0, -1, 1, 2)

    def second(group):
        for half in (0, 1):
            rows = pl.ds(*HALVES[half])

            def step(t, carry):
                k = row_of(offsets[group], t) if half == 0 else row_of(t, offsets[group])
                actg[rows] += dot(w2[k, rows], zr[k, :MAIN]) + dot(
                    w1[k, rows, MAIN:], zr[k, MAIN:]
                )
                return carry

            lax.fori_loop(0, side, step, 0)

    def whole(group):
        return [
            row_of(offsets[a], offsets[b])
            for a in range(group + 1)
            for b in range(group + 1)
            if max(a, b) == group
        ]

    waiting = []
    for group in range(4):
        end2[group]()
        second(group)
        if group < 3:
            for d in whole(group):
                forward_block(d)
            for d in waiting:
                sum_a.near(d)
            waiting = whole(group)

    v = pre[:, :TOK]
    tangent = tangent_of(v)
    slope = 0.5 * (1.0 + tangent) + 0.5 * v * (1.0 - tangent * tangent) * COEFF * (
        1.0 + 3.0 * CUBIC * v * v
    )
    grad = (actg[...] * slope).astype(BF16).astype(F32)
    split_store(pg_t, grad)

    extra = pre[:, TOK:]
    ones = extra[:, 4:5]
    scaled = ones + jnp.where(in_one, extra[:, 0:1], extra[:, 1:2])
    shifted = jnp.where(in_one, extra[:, 2:3], extra[:, 3:4])
    sums = jnp.concatenate(
        [
            jnp.sum(grad * scaled, axis=0, keepdims=True),
            jnp.sum(grad * (v - shifted), axis=0, keepdims=True),
            jnp.zeros((SUMS - 2, TOK), F32),
        ],
        axis=0,
    )

    def put_sums(k, carry):
        part_b[k, 0, FEAT:] = sums
        part_b[k, 1, FEAT:] = sums
        return carry

    lax.fori_loop(0, n_dev, put_sums, 0)

    def batch(far):
        return [wrap(z + way * (slot - 1 + 4 * far), n_dev) for slot in (3, 2, 0, 1)]

    def backward(steps):
        for step in steps:
            backward_block(wrap(z + step, n_dev))

    def near(far):
        for d in batch(far):
            sum_b.near(d)

    backward((10, 6, 9, 7, 8))
    near(2)
    for d in waiting:
        sum_a.near(d)
    backward((5, 11, 3, 13, 4, 12))
    near(1)
    sum_b.far(2)
    for d in whole(3):
        forward_block(d)
    backward((14, 2))
    near(3)
    for d in whole(3):
        sum_a.near(d)
    sum_b.far(1)
    sum_b.far(3)
    sum_a.far(2)
    backward((1, 15, 0))
    near(0)
    sum_a.far(1)
    sum_a.far(3)

    x = xg[z, core, :FEAT, :].astype(F32)
    normed = (x - centre) * inverse
    gate = local[0]
    g = local[1]
    mine = dot_tn(tile, pick[:, : 4 * TOK])
    scale_one = 1.0 + jnp.concatenate(
        [mine[:, :TOK], mine[: FEAT - TOK, 2 * TOK : 3 * TOK]], axis=0
    )
    lane_at = lax.broadcasted_iota(jnp.int32, (FEAT, TOK), 1)

    def put(lanes, index, value):
        a = jnp.sum(value * first_mask, axis=1, keepdims=True)
        b = jnp.sum(value * second_mask, axis=1, keepdims=True)
        lanes = jnp.where(lane_at == index, a, lanes)
        return jnp.where(lane_at == index + 1, b, lanes)

    projected = sum_a.last()
    block_out[...] = (live * (x + gate * projected)).astype(BF16)
    lanes = put(jnp.zeros((FEAT, TOK), F32), 16, projected * g)

    total = sum_b.last()
    mod_grad = total[:FEAT]
    first_mean = total[FEAT : FEAT + 1] / width
    second_mean = total[FEAT + 1 : FEAT + 2] / width
    norm_grad = mod_grad * scale_one
    input_out[...] = (
        live * (g + inverse * (norm_grad - first_mean - normed * second_mean))
    ).astype(BF16)
    lanes = put(lanes, 0, mod_grad)
    lanes = put(lanes, 8, mod_grad * normed)
    high, low = lanes[:TOK].T, lanes[TOK:].T
    for i in range(3):
        mod_out[i, :, :TOK] = high[8 * i : 8 * i + 2]
        mod_out[i, :, TOK:] = low[8 * i : 8 * i + 2]

    sum_a.sent()
    sum_b.sent()
    for copy in pending:
        copy.wait_send()


def body(hidden_states, clip_lengths, modulation, fc1_weight, fc2_weight, out_grad):
    depth = lax.axis_size("col") // 2
    side = 4
    vmem = pl.BlockSpec(memory_space=pltpu.VMEM)
    smem = pl.BlockSpec(memory_space=pltpu.SMEM)
    dma = pltpu.SemaphoreType.DMA
    block, grad, mods = pl.pallas_call(
        lambda *refs: kernel(depth, side, *refs),
        out_shape=(
            jax.ShapeDtypeStruct((FEAT, TOK), BF16),
            jax.ShapeDtypeStruct((FEAT, TOK), BF16),
            jax.ShapeDtypeStruct((3, 2, FEAT), F32),
        ),
        in_specs=[vmem, smem] + [vmem] * 4,
        out_specs=(vmem, vmem, vmem),
        scratch_shapes=[
            pltpu.VMEM((16, HID, WIDE), BF16),
            pltpu.VMEM((16, HID, MAIN), BF16),
            pltpu.VMEM((depth, 2, MSG, TOK), BF16),
            pltpu.VMEM((depth, WIDE, TOK), BF16),
            pltpu.VMEM((depth, WIDE, 2 * TOK), BF16),
            pltpu.VMEM((HID, 2 * TOK), F32),
            pltpu.VMEM((HID, TOK), F32),
            pltpu.VMEM((TOK, HID), BF16),
            pltpu.VMEM((TOK, HID), BF16),
            pltpu.VMEM((depth, 2, FEAT, TOK), F32),
            pltpu.VMEM((depth, FEAT, TOK), F32),
            pltpu.VMEM((depth, 2, FEAT + SUMS, TOK), F32),
            pltpu.VMEM((depth, FEAT + SUMS, TOK), F32),
            pltpu.VMEM((4, 4, FEAT, TOK), SUM_TYPE),
            pltpu.VMEM((4, 4, FEAT + SUMS, TOK), SUM_TYPE),
            pltpu.VMEM((4, 4, FEAT, TOK), SUM_TYPE),
            pltpu.VMEM((4, 4, FEAT + SUMS, TOK), SUM_TYPE),
            pltpu.VMEM((4, FEAT, TOK), SUM_TYPE),
            pltpu.VMEM((4, FEAT + SUMS, TOK), SUM_TYPE),
            pltpu.VMEM((4, FEAT, TOK), SUM_TYPE),
            pltpu.VMEM((4, FEAT + SUMS, TOK), SUM_TYPE),
            pltpu.VMEM((2, FEAT, TOK), F32),
            dma((2, 2, 5, 4)),
            dma((2, 2, 5, 4)),
            dma((2, 15)),
            dma((2, 15)),
            dma((2, depth)),
            dma((2, depth)),
            dma((2, depth)),
            dma((2, depth)),
            dma((2, 20)),
            dma((2, 20)),
        ],
        compiler_params=pltpu.CompilerParams(
            collective_id=0, has_side_effects=True, vmem_limit_bytes=60000 * 1024
        ),
    )(
        hidden_states.T,
        clip_lengths,
        modulation.transpose(1, 0, 2),
        fc1_weight,
        fc2_weight.T,
        out_grad.T,
    )
    return block.T, grad.T, mods.transpose(1, 0, 2)


def solution(mesh):
    return jax.shard_map(
        body,
        mesh=mesh,
        in_specs=(
            P("row", "col"),
            P("row", None),
            P("row", None, "col"),
            P("row", "col"),
            P("col", "row"),
            P("row", "col"),
        ),
        out_specs=(P("row", "col"), P("row", "col"), P("row", None, "col")),
        check_vma=False,
    )
```

```python
import jax
import jax.numpy as jnp
from jax import lax
from jax.experimental import pallas as pl
from jax.experimental.pallas import tpu as pltpu
from jax.sharding import PartitionSpec as P

EPSILON = 1e-06
COEFF = 0.7978845608028654
CUBIC = 0.044715
MESH = pl.DeviceIdType.MESH
F32 = jnp.float32
BF16 = jnp.bfloat16
SUM_TYPE = jnp.bfloat16

TOK = 128
FEAT = 160
HID = 432
ROWF = 320
MAIN = 256
REM = ROWF - MAIN
WIDE = MAIN + 2 * REM
QUARTERS = ((0, 112), (112, 112), (224, 112), (336, 96))
HALVES = ((0, 224), (224, 208))
MSG = FEAT + 16
SUMS = 16


def dot(a, b):
    return jnp.dot(a, b, preferred_element_type=F32)


def dot_tn(a, b):
    return lax.dot_general(a, b, (((0,), (0,)), ((), ())), preferred_element_type=F32)


def kernel(
    depth,
    side,
    hidden_in,
    lengths_in,
    mod_in,
    fc1_in,
    fc2_in,
    grad_in,
    block_out,
    input_out,
    mod_out,
    w1,
    w2,
    xg,
    zr,
    xm,
    pre,
    actg,
    act_t,
    pg_t,
    part_a,
    hand_a,
    part_b,
    hand_b,
    left_a,
    left_b,
    outl_a,
    outl_b,
    right_a,
    right_b,
    outr_a,
    outr_b,
    local,
    w_send,
    w_recv,
    z_send,
    z_recv,
    p_send,
    p_recv,
    h_send,
    h_recv,
    s_send,
    s_recv,
):
    n_dev = depth
    row = lax.axis_index("row")
    col = lax.axis_index("col")
    px, py = row // side, row % side
    z, core = col // 2, col % 2

    def wrap(value, size):
        return lax.rem(value + 2 * size, size)

    def row_of(dx, dy):
        return wrap(px + dx, side) * side + wrap(py + dy, side)

    def col_of(dz):
        return wrap(z + dz, n_dev) * 2 + core

    def at_row(dx, dy):
        return (row_of(dx, dy), col)

    way = 1 - 2 * core

    def at_col(dz):
        return (row, col_of(way * dz))

    partner = (row, z * 2 + (1 - core))
    neighbours = [
        at_row(1, 0),
        at_row(-1, 0),
        at_row(0, 1),
        at_row(0, -1),
        partner,
    ] + [at_col(step) for step in (1, -1, 2, -2, 4, -4)]

    barrier = pltpu.get_barrier_semaphore()
    for device in neighbours:
        pl.semaphore_signal(barrier, inc=1, device_id=device, device_id_type=MESH)

    def clear(k, carry):
        zr[k, ROWF:, :] = jnp.zeros((REM, TOK), BF16)
        xm[k, MAIN:ROWF, :] = jnp.zeros((REM, 2 * TOK), BF16)
        return carry

    def flip(value):
        return value.astype(F32).T

    def own_weights(start, size):
        at = pl.ds(start, size)
        for f in range(0, MAIN, TOK):
            w1[row, at, f : f + TOK] = flip(fc1_in[f : f + TOK, at]).astype(BF16)
            w2[row, at, f : f + TOK] = flip(fc2_in[f : f + TOK, at]).astype(BF16)
        both = jnp.concatenate([fc2_in[MAIN:, at], fc1_in[MAIN:, at]], axis=0)
        w1[row, at, MAIN:] = flip(both).astype(BF16)

    for start in range(0, HID, TOK):
        own_weights(start, min(TOK, HID - start))
    pl.semaphore_wait(barrier, len(neighbours))

    pending = []

    def send(ref, at, device, ssem, rsem):
        copy = pltpu.make_async_remote_copy(
            src_ref=ref.at[at],
            dst_ref=ref.at[at],
            send_sem=ssem,
            recv_sem=rsem,
            device_id=device,
            device_id_type=MESH,
        )
        copy.start()
        pending.append(copy)

    def arrive(ref, at, device, ssem, rsem):
        pltpu.make_async_remote_copy(
            src_ref=ref.at[at],
            dst_ref=ref.at[at],
            send_sem=ssem,
            recv_sem=rsem,
            device_id=device,
            device_id_type=MESH,
        ).wait_recv()

    class Ring:
        def __init__(self, weight, half, group, base, along):
            self.ref = (w1, w2)[weight]
            self.weight, self.half, self.group = weight, half, group
            self.base, self.along = base, along

        def slot(self, offset):
            dx, dy = self.base
            if self.along == 0:
                return row_of(dx + offset, dy)
            return row_of(dx, dy + offset)

        def peer(self, offset):
            return at_row(offset, 0) if self.along == 0 else at_row(0, offset)

        def sems(self, i):
            at = (self.weight, self.half, self.group, i)
            return w_send.at[at], w_recv.at[at]

        def rows(self, quarter):
            if quarter is None:
                return pl.ds(*HALVES[self.half])
            return pl.ds(*QUARTERS[2 * self.half + quarter])

        def move(self, fn, offset, quarter, to, i):
            fn(self.ref, (self.slot(offset), self.rows(quarter)), self.peer(to), *self.sems(i))

        def start(self):
            self.move(send, 0, None, 1, 0)
            self.move(send, 0, None, -1, 1)

        def middle(self, side_of):
            if side_of < 0:
                self.move(arrive, -1, None, -1, 0)
                self.move(send, -1, 0, 1, 2)
            else:
                self.move(arrive, 1, None, 1, 1)
                self.move(send, 1, 1, -1, 3)

        def end(self):
            self.move(arrive, 2, 0, -1, 2)
            self.move(arrive, 2, 1, 1, 3)

    def rings_of(weight):
        first, second = [], []
        for half in (0, 1):
            first.append(Ring(weight, half, 0, (0, 0), half))
            for i, offset in enumerate((0, -1, 1, 2)):
                base = (offset, 0) if half == 0 else (0, offset)
                second.append(Ring(weight, half, 1 + i, base, 1 - half))
        return first, second

    def weight_steps(weight):
        first, second = rings_of(weight)

        def begin():
            for ring in first:
                ring.start()
            second[0].start()
            second[4].start()

        def near():
            for half in (0, 1):
                first[half].middle(-1)
                second[4 * half + 1].start()
            for half in (0, 1):
                first[half].middle(1)
                second[4 * half + 2].start()

        def far():
            for half in (0, 1):
                first[half].end()
                second[4 * half + 3].start()

        def pass_on(i):
            def act():
                for half in (0, 1):
                    second[4 * half + i].middle(-1)
                    second[4 * half + i].middle(1)

            return act

        def finish(i):
            def act():
                for half in (0, 1):
                    second[4 * half + i].end()

            return act

        return begin, near, far, [pass_on(i) for i in range(4)], [finish(i) for i in range(4)]

    begin1, near1, far1, pass1, end1 = weight_steps(0)
    begin2, near2, far2, pass2, end2 = weight_steps(1)

    def message(m, dz, who):
        k = wrap(z + (way if who is core else -way) * dz, n_dev)
        if m == 0:
            return xg, (k, who)
        return zr, (k, pl.ds(pl.multiple_of(who * FEAT, FEAT), FEAT))

    def hand_over(m, dz, i):
        ref, at = message(m, dz, core)
        send(ref, at, partner, p_send.at[m, i], p_recv.at[m, i])

    near_by = (1, -1, 2)
    bases = (0, -4, 4, 8)

    def base(j):
        return bases[j]

    def spread(m, j):
        ref, at = message(m, base(j), core)
        for i, step in enumerate(near_by):
            n = 3 + 3 * j + i
            send(ref, at, at_col(step), z_send.at[m, n], z_recv.at[m, n])

    def z_begin(m):
        ref, at = message(m, 0, core)
        for n, step in ((0, 4), (1, -4)):
            send(ref, at, at_col(step), z_send.at[m, n], z_recv.at[m, n])
        spread(m, 0)
        hand_over(m, 0, 0)

    def z_jump(m):
        ref, at = message(m, -4, core)
        arrive(ref, at, at_col(-4), z_send.at[m, 0], z_recv.at[m, 0])
        send(ref, at, at_col(4), z_send.at[m, 2], z_recv.at[m, 2])
        spread(m, 1)
        hand_over(m, -4, 1)
        ref, at = message(m, 4, core)
        arrive(ref, at, at_col(4), z_send.at[m, 1], z_recv.at[m, 1])
        spread(m, 2)
        hand_over(m, 4, 2)

    def z_jump_far(m):
        ref, at = message(m, -8, core)
        arrive(ref, at, at_col(-4), z_send.at[m, 2], z_recv.at[m, 2])
        spread(m, 3)
        hand_over(m, 8, 3)

    def z_near(m, j):
        for i, step in enumerate(near_by):
            n = 3 + 3 * j + i
            ref, at = message(m, base(j) - step, core)
            arrive(ref, at, at_col(-step), z_send.at[m, n], z_recv.at[m, n])
            hand_over(m, base(j) - step, 4 + 3 * j + i)

    def z_handed(m):
        for j in range(4):
            for i in range(4):
                offset = base(j) - ((0,) + near_by)[i]
                n = j if i == 0 else 3 + 3 * j + i
                ref, at = message(m, offset, 1 - core)
                arrive(ref, at, partner, p_send.at[m, n], p_recv.at[m, n])

    begin1()

    lane = lax.broadcasted_iota(jnp.int32, (1, TOK), 1)
    end_one = lengths_in[0, 0]
    end_two = end_one + lengths_in[0, 1]
    ones_row = jnp.ones((1, TOK), F32)
    zero_row = jnp.zeros((1, TOK), F32)
    in_one = lane < end_one
    first_mask = jnp.where(in_one, ones_row, zero_row)
    live = jnp.where(lane < end_two, ones_row, zero_row)
    second_mask = live - first_mask

    xg[z, core, :FEAT, :] = hidden_in[...]
    mods = [mod_in[i].astype(F32) for i in range(3)]
    at_row8 = lax.broadcasted_iota(jnp.int32, (8, FEAT), 0)
    rows = jnp.where(at_row8 == 4, 1.0, jnp.zeros((8, FEAT), F32))
    for i, source in enumerate((1, 0)):
        rows = jnp.where(at_row8 == 2 * i, mods[source][0:1], rows)
        rows = jnp.where(at_row8 == 2 * i + 1, mods[source][1:2], rows)
    rows = jnp.where(at_row8 == 5, mods[2][0:1], rows)
    rows = jnp.where(at_row8 == 6, mods[2][1:2], rows)
    tail = lax.broadcasted_iota(jnp.int32, (FEAT, TOK), 0) - TOK
    shift_lanes = jnp.where(
        tail == lax.broadcasted_iota(jnp.int32, (FEAT, TOK), 1),
        jnp.ones((FEAT, TOK), F32),
        jnp.zeros((FEAT, TOK), F32),
    ).astype(BF16)
    tile = jnp.concatenate([rows[:, :TOK], dot(rows.astype(BF16), shift_lanes)], axis=0).astype(BF16)
    xg[z, core, FEAT:, :] = tile

    pick_row = lax.broadcasted_iota(jnp.int32, (16, TOK), 0)
    pick_lane = lax.broadcasted_iota(jnp.int32, (16, TOK), 1)
    pick_zero = jnp.zeros((16, TOK), F32)

    def picker(at):
        low = jnp.where(pick_row == at + 1, second_mask, pick_zero)
        return jnp.where(pick_row == at, first_mask, low)

    def lanes_of(base):
        inside = (pick_row - base == pick_lane) & (pick_lane < 8)
        return jnp.where(inside, 1.0, pick_zero)

    pick = jnp.concatenate(
        [picker(0), picker(2), picker(8), picker(10), lanes_of(0), lanes_of(8)], axis=1
    ).astype(BF16)
    pick_gate = jnp.concatenate([picker(5), picker(13)], axis=1).astype(BF16)
    gates = dot_tn(tile, pick_gate)
    gate_here = jnp.concatenate([gates[:, :TOK], gates[: FEAT - TOK, TOK:]], axis=0)
    g_here = grad_in[...].astype(F32)
    local[0] = gate_here
    local[1] = g_here
    zr[z, pl.ds(pl.multiple_of(core * FEAT, FEAT), FEAT), :] = (live * gate_here * g_here).astype(
        BF16
    )
    z_begin(0)
    z_begin(1)
    lax.fori_loop(0, n_dev, clear, 0)
    near1()
    z_jump(0)
    far1()
    begin2()
    pass1[0]()
    z_jump_far(0)
    z_jump(1)
    z_near(0, 0)
    pass1[1]()
    z_near(0, 1)
    z_near(0, 2)
    pass1[2]()
    z_jump_far(1)
    z_near(0, 3)
    pass1[3]()
    z_handed(0)
    near2()

    def add_up(k, carry):
        x = xg[k, :, :FEAT, :].astype(F32)
        return carry + jnp.sum(x.reshape(2 * FEAT, TOK), axis=0, keepdims=True)

    width = n_dev * 2 * FEAT
    centre = lax.fori_loop(0, n_dev, add_up, jnp.zeros((1, TOK), F32)) / width

    def add_square(k, carry):
        x = xg[k, :, :FEAT, :].astype(F32).reshape(2 * FEAT, TOK) - centre
        return carry + jnp.sum(x * x, axis=0, keepdims=True)

    spread = lax.fori_loop(0, n_dev, add_square, jnp.zeros((1, TOK), F32)) / width
    inverse = lax.rsqrt(spread + EPSILON)

    far2()
    def modulate(k, carry):
        for j in (0, 1):
            x = (xg[k, j, :FEAT, :].astype(F32) - centre) * inverse
            wide = dot_tn(xg[k, j, FEAT:, :], pick)
            top = (x[:TOK] * (1.0 + wide[:, :TOK]) + wide[:, TOK : 2 * TOK]).astype(BF16)
            low = wide[: FEAT - TOK]
            rest = (x[TOK:] * (1.0 + low[:, 2 * TOK : 3 * TOK]) + low[:, 3 * TOK : 4 * TOK]).astype(
                BF16
            )
            top_mod = wide[:, 4 * TOK : 5 * TOK].astype(BF16)
            rest_mod = low[:, 5 * TOK :].astype(BF16)
            if j == 0:
                xm[k, 0:128, 0:TOK] = top
                xm[k, 128:160, 0:TOK] = rest
                xm[k, 0:128, TOK:] = top_mod
                xm[k, 128:160, TOK:] = rest_mod
            else:
                xm[k, 160:256, 0:TOK] = top[:96]
                xm[k, 320:352, 0:TOK] = top[96:]
                xm[k, 352:384, 0:TOK] = rest
                xm[k, 160:256, TOK:] = top_mod[:96]
                xm[k, 320:352, TOK:] = top_mod[96:]
                xm[k, 352:384, TOK:] = rest_mod
        return carry

    lax.fori_loop(0, n_dev // 2, modulate, 0)
    z_near(1, 0)
    z_near(1, 1)
    pass2[0]()
    lax.fori_loop(n_dev // 2, n_dev, modulate, 0)
    z_near(1, 2)
    z_near(1, 3)
    pass2[1]()
    for act in end1:
        act()

    pre[...] = jnp.zeros((HID, 2 * TOK), F32)

    def first(k, carry):
        pre[...] += dot(w1[k], xm[k])
        return carry

    lax.fori_loop(0, n_dev // 2, first, 0)
    pass2[2]()
    lax.fori_loop(n_dev // 2, n_dev, first, 0)
    pass2[3]()
    z_handed(1)

    def tangent_of(v):
        return jnp.tanh(COEFF * (v + CUBIC * v * v * v))

    def split_store(ref, value):
        for start in range(0, HID, TOK):
            stop = min(start + TOK, HID)
            ref[:, start:stop] = value[start:stop].T.astype(BF16)

    v = pre[:, :TOK]
    split_store(act_t, 0.5 * v * (1.0 + tangent_of(v)))

    half_z = n_dev // 2

    class Sum:
        def __init__(self, i, part, hand, left, outl, right, outr):
            self.i = i
            self.part, self.hand = part, hand
            self.land, self.out = (left, right), (outl, outr)

        def owner(self, side_of, s):
            return wrap(z - half_z - 1 + s if side_of == 0 else z + half_z - s, n_dev)

        def hand_over(self, d):
            copy = pltpu.make_async_remote_copy(
                src_ref=self.part.at[d, 1 - core],
                dst_ref=self.hand.at[d],
                send_sem=h_send.at[self.i, d],
                recv_sem=h_recv.at[self.i, d],
                device_id=partner,
                device_id_type=MESH,
            )
            copy.start()
            pending.append(copy)

        def both_cores(self, d):
            arrive(self.hand, d, partner, h_send.at[self.i, d], h_recv.at[self.i, d])
            return self.part[d, core] + self.hand[d]

        def link(self, side_of, s):
            return pltpu.make_async_remote_copy(
                src_ref=self.out[side_of].at[s - 1],
                dst_ref=self.land[side_of].at[s - 1],
                send_sem=s_send.at[self.i, side_of, s - 1],
                recv_sem=s_recv.at[self.i, side_of, s - 1],
                device_id=(row, col_of(-1 if side_of == 0 else 1)),
                device_id_type=MESH,
            )

        def from_chain(self, side_of, s):
            self.link(side_of, s).wait_recv()
            return self.land[side_of][s - 1].astype(F32)

        def step(self, s):
            for side_of in (0, 1):
                if side_of == 1 and s == half_z:
                    continue
                total = self.both_cores(self.owner(side_of, s))
                if s > 1:
                    total = total + self.from_chain(side_of, s - 1)
                self.out[side_of][s - 1] = total.astype(SUM_TYPE)
                copy = self.link(side_of, s)
                copy.start()
                pending.append(copy)

        def last(self):
            total = self.both_cores(z)
            total = total + self.from_chain(0, half_z)
            return total + self.from_chain(1, half_z - 1)

    sum_a = Sum(0, part_a, hand_a, left_a, outl_a, right_a, outr_a)
    sum_b = Sum(1, part_b, hand_b, left_b, outl_b, right_b, outr_b)

    def forward_block(d):
        acted = act_t[...]
        main = dot(acted, w2[d]).T
        rest = dot(acted, w1[d, :, MAIN:]).T
        part_a[d, 0] = main[:FEAT]
        part_a[d, 1, : MAIN - FEAT] = main[FEAT:]
        part_a[d, 1, MAIN - FEAT :] = rest[:REM]
        sum_a.hand_over(d)

    def backward_block(d):
        both = dot(pg_t[...], w1[d])
        main = both[:, :MAIN].T
        rest = both[:, MAIN:].T
        part_b[d, 0, :FEAT] = main[:FEAT]
        part_b[d, 1, : MAIN - FEAT] = main[FEAT:]
        part_b[d, 1, MAIN - FEAT : FEAT] = rest[REM:]
        sum_b.hand_over(d)

    actg[...] = jnp.zeros((HID, TOK), F32)
    offsets = (0, -1, 1, 2)

    def second(group):
        for half in (0, 1):
            rows = pl.ds(*HALVES[half])

            def step(t, carry):
                k = row_of(offsets[group], t) if half == 0 else row_of(t, offsets[group])
                actg[rows] += dot(w2[k, rows], zr[k, :MAIN]) + dot(
                    w1[k, rows, MAIN:], zr[k, MAIN:]
                )
                return carry

            lax.fori_loop(0, side, step, 0)

    def whole(group):
        return [
            row_of(offsets[a], offsets[b])
            for a in range(group + 1)
            for b in range(group + 1)
            if max(a, b) == group
        ]

    for group in range(4):
        end2[group]()
        second(group)
        if group < 3:
            for d in whole(group):
                forward_block(d)

    v = pre[:, :TOK]
    tangent = tangent_of(v)
    slope = 0.5 * (1.0 + tangent) + 0.5 * v * (1.0 - tangent * tangent) * COEFF * (
        1.0 + 3.0 * CUBIC * v * v
    )
    grad = (actg[...] * slope).astype(BF16).astype(F32)
    split_store(pg_t, grad)

    extra = pre[:, TOK:]
    ones = extra[:, 4:5]
    scaled = ones + jnp.where(in_one, extra[:, 0:1], extra[:, 1:2])
    shifted = jnp.where(in_one, extra[:, 2:3], extra[:, 3:4])
    sums = jnp.concatenate(
        [
            jnp.sum(grad * scaled, axis=0, keepdims=True),
            jnp.sum(grad * (v - shifted), axis=0, keepdims=True),
            jnp.zeros((SUMS - 2, TOK), F32),
        ],
        axis=0,
    )

    def put_sums(k, carry):
        part_b[k, 0, FEAT:] = sums
        part_b[k, 1, FEAT:] = sums
        return carry

    lax.fori_loop(0, n_dev, put_sums, 0)

    def backward(s):
        if s <= half_z:
            backward_block(sum_b.owner(0, s))
            backward_block(sum_b.owner(1, s) if s < half_z else z)

    rest = whole(3)
    backward(1)
    for d in rest[:3]:
        forward_block(d)
    sum_b.step(1)
    for d in rest[3:]:
        forward_block(d)
    backward(2)
    sum_a.step(1)
    for s in range(2, half_z + 1):
        sum_b.step(s)
        backward(s + 1)
        sum_a.step(s)

    x = xg[z, core, :FEAT, :].astype(F32)
    normed = (x - centre) * inverse
    gate = local[0]
    g = local[1]
    mine = dot_tn(tile, pick[:, : 4 * TOK])
    scale_one = 1.0 + jnp.concatenate(
        [mine[:, :TOK], mine[: FEAT - TOK, 2 * TOK : 3 * TOK]], axis=0
    )
    lane_at = lax.broadcasted_iota(jnp.int32, (FEAT, TOK), 1)

    def put(lanes, index, value):
        a = jnp.sum(value * first_mask, axis=1, keepdims=True)
        b = jnp.sum(value * second_mask, axis=1, keepdims=True)
        lanes = jnp.where(lane_at == index, a, lanes)
        return jnp.where(lane_at == index + 1, b, lanes)

    projected = sum_a.last()
    block_out[...] = (live * (x + gate * projected)).astype(BF16)
    lanes = put(jnp.zeros((FEAT, TOK), F32), 16, projected * g)

    total = sum_b.last()
    mod_grad = total[:FEAT]
    first_mean = total[FEAT : FEAT + 1] / width
    second_mean = total[FEAT + 1 : FEAT + 2] / width
    norm_grad = mod_grad * scale_one
    input_out[...] = (
        live * (g + inverse * (norm_grad - first_mean - normed * second_mean))
    ).astype(BF16)
    lanes = put(lanes, 0, mod_grad)
    lanes = put(lanes, 8, mod_grad * normed)
    high, low = lanes[:TOK].T, lanes[TOK:].T
    for i in range(3):
        mod_out[i, :, :TOK] = high[8 * i : 8 * i + 2]
        mod_out[i, :, TOK:] = low[8 * i : 8 * i + 2]

    for copy in pending:
        copy.wait_send()


def body(hidden_states, clip_lengths, modulation, fc1_weight, fc2_weight, out_grad):
    depth = lax.axis_size("col") // 2
    side = 4
    vmem = pl.BlockSpec(memory_space=pltpu.VMEM)
    smem = pl.BlockSpec(memory_space=pltpu.SMEM)
    dma = pltpu.SemaphoreType.DMA
    block, grad, mods = pl.pallas_call(
        lambda *refs: kernel(depth, side, *refs),
        out_shape=(
            jax.ShapeDtypeStruct((FEAT, TOK), BF16),
            jax.ShapeDtypeStruct((FEAT, TOK), BF16),
            jax.ShapeDtypeStruct((3, 2, FEAT), F32),
        ),
        in_specs=[vmem, smem] + [vmem] * 4,
        out_specs=(vmem, vmem, vmem),
        scratch_shapes=[
            pltpu.VMEM((16, HID, WIDE), BF16),
            pltpu.VMEM((16, HID, MAIN), BF16),
            pltpu.VMEM((depth, 2, MSG, TOK), BF16),
            pltpu.VMEM((depth, WIDE, TOK), BF16),
            pltpu.VMEM((depth, WIDE, 2 * TOK), BF16),
            pltpu.VMEM((HID, 2 * TOK), F32),
            pltpu.VMEM((HID, TOK), F32),
            pltpu.VMEM((TOK, HID), BF16),
            pltpu.VMEM((TOK, HID), BF16),
            pltpu.VMEM((depth, 2, FEAT, TOK), F32),
            pltpu.VMEM((depth, FEAT, TOK), F32),
            pltpu.VMEM((depth, 2, FEAT + SUMS, TOK), F32),
            pltpu.VMEM((depth, FEAT + SUMS, TOK), F32),
            pltpu.VMEM((depth // 2, FEAT, TOK), SUM_TYPE),
            pltpu.VMEM((depth // 2, FEAT + SUMS, TOK), SUM_TYPE),
            pltpu.VMEM((depth // 2, FEAT, TOK), SUM_TYPE),
            pltpu.VMEM((depth // 2, FEAT + SUMS, TOK), SUM_TYPE),
            pltpu.VMEM((depth // 2, FEAT, TOK), SUM_TYPE),
            pltpu.VMEM((depth // 2, FEAT + SUMS, TOK), SUM_TYPE),
            pltpu.VMEM((depth // 2, FEAT, TOK), SUM_TYPE),
            pltpu.VMEM((depth // 2, FEAT + SUMS, TOK), SUM_TYPE),
            pltpu.VMEM((2, FEAT, TOK), F32),
            dma((2, 2, 5, 4)),
            dma((2, 2, 5, 4)),
            dma((2, 15)),
            dma((2, 15)),
            dma((2, depth)),
            dma((2, depth)),
            dma((2, depth)),
            dma((2, depth)),
            dma((2, 2, depth // 2)),
            dma((2, 2, depth // 2)),
        ],
        compiler_params=pltpu.CompilerParams(
            collective_id=0, has_side_effects=True, vmem_limit_bytes=60000 * 1024
        ),
    )(
        hidden_states.T,
        clip_lengths,
        modulation.transpose(1, 0, 2),
        fc1_weight,
        fc2_weight.T,
        out_grad.T,
    )
    return block.T, grad.T, mods.transpose(1, 0, 2)


def solution(mesh):
    return jax.shard_map(
        body,
        mesh=mesh,
        in_specs=(
            P("row", "col"),
            P("row", None),
            P("row", None, "col"),
            P("row", "col"),
            P("col", "row"),
            P("row", "col"),
        ),
        out_specs=(P("row", "col"), P("row", "col"), P("row", None, "col")),
        check_vma=False,
    )
```

```python
import jax
import jax.numpy as jnp
from jax import lax
from jax.experimental import pallas as pl
from jax.experimental.pallas import tpu as pltpu
from jax.sharding import PartitionSpec as P

EPSILON = 1e-06
COEFF = 0.7978845608028654
CUBIC = 0.044715
MESH = pl.DeviceIdType.MESH
F32 = jnp.float32
BF16 = jnp.bfloat16
SUM_TYPE = jnp.bfloat16

TOK = 128
FEAT = 160
HID = 432
ROWF = 320
MAIN = 256
REM = ROWF - MAIN
WIDE = MAIN + 2 * REM
QUARTERS = ((0, 112), (112, 112), (224, 112), (336, 96))
HALVES = ((0, 224), (224, 208))
MSG = FEAT + 16
SUMS = 16


def dot(a, b):
    return jnp.dot(a, b, preferred_element_type=F32)


def dot_tn(a, b):
    return lax.dot_general(a, b, (((0,), (0,)), ((), ())), preferred_element_type=F32)


def kernel(
    depth,
    side,
    hidden_in,
    lengths_in,
    mod_in,
    fc1_in,
    fc2_in,
    grad_in,
    block_out,
    input_out,
    mod_out,
    w1,
    w2,
    xg,
    zr,
    xm,
    pre,
    actg,
    act_t,
    pg_t,
    part_a,
    hand_a,
    part_b,
    hand_b,
    left_a,
    left_b,
    outl_a,
    outl_b,
    right_a,
    right_b,
    outr_a,
    outr_b,
    local,
    w_send,
    w_recv,
    z_send,
    z_recv,
    p_send,
    p_recv,
    h_send,
    h_recv,
    s_send,
    s_recv,
):
    n_dev = depth
    row = lax.axis_index("row")
    col = lax.axis_index("col")
    px, py = row // side, row % side
    z, core = col // 2, col % 2

    def wrap(value, size):
        return lax.rem(value + 2 * size, size)

    def row_of(dx, dy):
        return wrap(px + dx, side) * side + wrap(py + dy, side)

    def col_of(dz):
        return wrap(z + dz, n_dev) * 2 + core

    def at_row(dx, dy):
        return (row_of(dx, dy), col)

    way = 1 - 2 * core

    def at_col(dz):
        return (row, col_of(way * dz))

    partner = (row, z * 2 + (1 - core))
    neighbours = [
        at_row(1, 0),
        at_row(-1, 0),
        at_row(0, 1),
        at_row(0, -1),
        partner,
    ] + [at_col(step) for step in (1, -1, 2, -2, 4, -4)]

    barrier = pltpu.get_barrier_semaphore()
    for device in neighbours:
        pl.semaphore_signal(barrier, inc=1, device_id=device, device_id_type=MESH)

    def clear(k, carry):
        zr[k, ROWF:, :] = jnp.zeros((REM, TOK), BF16)
        xm[k, MAIN:ROWF, :] = jnp.zeros((REM, 2 * TOK), BF16)
        return carry

    def flip(value):
        return value.astype(F32).T

    def own_weights(start, size):
        at = pl.ds(start, size)
        for f in range(0, MAIN, TOK):
            w1[row, at, f : f + TOK] = flip(fc1_in[f : f + TOK, at]).astype(BF16)
            w2[row, at, f : f + TOK] = flip(fc2_in[f : f + TOK, at]).astype(BF16)
        both = jnp.concatenate([fc2_in[MAIN:, at], fc1_in[MAIN:, at]], axis=0)
        w1[row, at, MAIN:] = flip(both).astype(BF16)

    for start in range(0, HID, TOK):
        own_weights(start, min(TOK, HID - start))
    pl.semaphore_wait(barrier, len(neighbours))

    pending = []

    def send(ref, at, device, ssem, rsem):
        copy = pltpu.make_async_remote_copy(
            src_ref=ref.at[at],
            dst_ref=ref.at[at],
            send_sem=ssem,
            recv_sem=rsem,
            device_id=device,
            device_id_type=MESH,
        )
        copy.start()
        pending.append(copy)

    def arrive(ref, at, device, ssem, rsem):
        pltpu.make_async_remote_copy(
            src_ref=ref.at[at],
            dst_ref=ref.at[at],
            send_sem=ssem,
            recv_sem=rsem,
            device_id=device,
            device_id_type=MESH,
        ).wait_recv()

    class Ring:
        def __init__(self, weight, half, group, base, along):
            self.ref = (w1, w2)[weight]
            self.weight, self.half, self.group = weight, half, group
            self.base, self.along = base, along

        def slot(self, offset):
            dx, dy = self.base
            if self.along == 0:
                return row_of(dx + offset, dy)
            return row_of(dx, dy + offset)

        def peer(self, offset):
            return at_row(offset, 0) if self.along == 0 else at_row(0, offset)

        def sems(self, i):
            at = (self.weight, self.half, self.group, i)
            return w_send.at[at], w_recv.at[at]

        def rows(self, quarter):
            if quarter is None:
                return pl.ds(*HALVES[self.half])
            return pl.ds(*QUARTERS[2 * self.half + quarter])

        def move(self, fn, offset, quarter, to, i):
            fn(self.ref, (self.slot(offset), self.rows(quarter)), self.peer(to), *self.sems(i))

        def start(self):
            self.move(send, 0, None, 1, 0)
            self.move(send, 0, None, -1, 1)

        def middle(self, side_of):
            if side_of < 0:
                self.move(arrive, -1, None, -1, 0)
                self.move(send, -1, 0, 1, 2)
            else:
                self.move(arrive, 1, None, 1, 1)
                self.move(send, 1, 1, -1, 3)

        def end(self):
            self.move(arrive, 2, 0, -1, 2)
            self.move(arrive, 2, 1, 1, 3)

    def rings_of(weight):
        first, second = [], []
        for half in (0, 1):
            first.append(Ring(weight, half, 0, (0, 0), half))
            for i, offset in enumerate((0, -1, 1, 2)):
                base = (offset, 0) if half == 0 else (0, offset)
                second.append(Ring(weight, half, 1 + i, base, 1 - half))
        return first, second

    def weight_steps(weight):
        first, second = rings_of(weight)

        def begin():
            for ring in first:
                ring.start()
            second[0].start()
            second[4].start()

        def near():
            for half in (0, 1):
                first[half].middle(-1)
                second[4 * half + 1].start()
            for half in (0, 1):
                first[half].middle(1)
                second[4 * half + 2].start()

        def far():
            for half in (0, 1):
                first[half].end()
                second[4 * half + 3].start()

        def pass_on(i):
            def act():
                for half in (0, 1):
                    second[4 * half + i].middle(-1)
                    second[4 * half + i].middle(1)

            return act

        def finish(i):
            def act():
                for half in (0, 1):
                    second[4 * half + i].end()

            return act

        return begin, near, far, [pass_on(i) for i in range(4)], [finish(i) for i in range(4)]

    begin1, near1, far1, pass1, end1 = weight_steps(0)
    begin2, near2, far2, pass2, end2 = weight_steps(1)

    def message(m, dz, who):
        k = wrap(z + (way if who is core else -way) * dz, n_dev)
        if m == 0:
            return xg, (k, who)
        return zr, (k, pl.ds(pl.multiple_of(who * FEAT, FEAT), FEAT))

    def hand_over(m, dz, i):
        ref, at = message(m, dz, core)
        send(ref, at, partner, p_send.at[m, i], p_recv.at[m, i])

    near_by = (1, -1, 2)
    bases = (0, -4, 4, 8)

    def base(j):
        return bases[j]

    def spread(m, j):
        ref, at = message(m, base(j), core)
        for i, step in enumerate(near_by):
            n = 3 + 3 * j + i
            send(ref, at, at_col(step), z_send.at[m, n], z_recv.at[m, n])

    def z_begin(m):
        ref, at = message(m, 0, core)
        for n, step in ((0, 4), (1, -4)):
            send(ref, at, at_col(step), z_send.at[m, n], z_recv.at[m, n])
        spread(m, 0)
        hand_over(m, 0, 0)

    def z_jump(m):
        ref, at = message(m, -4, core)
        arrive(ref, at, at_col(-4), z_send.at[m, 0], z_recv.at[m, 0])
        send(ref, at, at_col(4), z_send.at[m, 2], z_recv.at[m, 2])
        spread(m, 1)
        hand_over(m, -4, 1)
        ref, at = message(m, 4, core)
        arrive(ref, at, at_col(4), z_send.at[m, 1], z_recv.at[m, 1])
        spread(m, 2)
        hand_over(m, 4, 2)

    def z_jump_far(m):
        ref, at = message(m, -8, core)
        arrive(ref, at, at_col(-4), z_send.at[m, 2], z_recv.at[m, 2])
        spread(m, 3)
        hand_over(m, 8, 3)

    def z_near(m, j):
        for i, step in enumerate(near_by):
            n = 3 + 3 * j + i
            ref, at = message(m, base(j) - step, core)
            arrive(ref, at, at_col(-step), z_send.at[m, n], z_recv.at[m, n])
            hand_over(m, base(j) - step, 4 + 3 * j + i)

    def z_handed(m):
        for j in range(4):
            for i in range(4):
                offset = base(j) - ((0,) + near_by)[i]
                n = j if i == 0 else 3 + 3 * j + i
                ref, at = message(m, offset, 1 - core)
                arrive(ref, at, partner, p_send.at[m, n], p_recv.at[m, n])

    begin1()

    lane = lax.broadcasted_iota(jnp.int32, (1, TOK), 1)
    end_one = lengths_in[0, 0]
    end_two = end_one + lengths_in[0, 1]
    ones_row = jnp.ones((1, TOK), F32)
    zero_row = jnp.zeros((1, TOK), F32)
    in_one = lane < end_one
    first_mask = jnp.where(in_one, ones_row, zero_row)
    live = jnp.where(lane < end_two, ones_row, zero_row)
    second_mask = live - first_mask

    xg[z, core, :FEAT, :] = hidden_in[...]
    mods = [mod_in[i].astype(F32) for i in range(3)]
    at_row8 = lax.broadcasted_iota(jnp.int32, (8, FEAT), 0)
    rows = jnp.where(at_row8 == 4, 1.0, jnp.zeros((8, FEAT), F32))
    for i, source in enumerate((1, 0)):
        rows = jnp.where(at_row8 == 2 * i, mods[source][0:1], rows)
        rows = jnp.where(at_row8 == 2 * i + 1, mods[source][1:2], rows)
    rows = jnp.where(at_row8 == 5, mods[2][0:1], rows)
    rows = jnp.where(at_row8 == 6, mods[2][1:2], rows)
    tail = lax.broadcasted_iota(jnp.int32, (FEAT, TOK), 0) - TOK
    shift_lanes = jnp.where(
        tail == lax.broadcasted_iota(jnp.int32, (FEAT, TOK), 1),
        jnp.ones((FEAT, TOK), F32),
        jnp.zeros((FEAT, TOK), F32),
    ).astype(BF16)
    tile = jnp.concatenate([rows[:, :TOK], dot(rows.astype(BF16), shift_lanes)], axis=0).astype(BF16)
    xg[z, core, FEAT:, :] = tile

    pick_row = lax.broadcasted_iota(jnp.int32, (16, TOK), 0)
    pick_lane = lax.broadcasted_iota(jnp.int32, (16, TOK), 1)
    pick_zero = jnp.zeros((16, TOK), F32)

    def picker(at):
        low = jnp.where(pick_row == at + 1, second_mask, pick_zero)
        return jnp.where(pick_row == at, first_mask, low)

    def lanes_of(base):
        inside = (pick_row - base == pick_lane) & (pick_lane < 8)
        return jnp.where(inside, 1.0, pick_zero)

    pick = jnp.concatenate(
        [picker(0), picker(2), picker(8), picker(10), lanes_of(0), lanes_of(8)], axis=1
    ).astype(BF16)
    pick_gate = jnp.concatenate([picker(5), picker(13)], axis=1).astype(BF16)
    gates = dot_tn(tile, pick_gate)
    gate_here = jnp.concatenate([gates[:, :TOK], gates[: FEAT - TOK, TOK:]], axis=0)
    g_here = grad_in[...].astype(F32)
    local[0] = gate_here
    local[1] = g_here
    zr[z, pl.ds(pl.multiple_of(core * FEAT, FEAT), FEAT), :] = (live * gate_here * g_here).astype(
        BF16
    )
    z_begin(0)
    lax.fori_loop(0, n_dev, clear, 0)
    near1()
    z_jump(0)
    far1()
    begin2()
    pass1[0]()
    z_jump_far(0)
    z_begin(1)
    z_near(0, 0)
    pass1[1]()
    z_near(0, 1)
    z_near(0, 2)
    z_jump(1)
    pass1[2]()
    z_near(0, 3)
    pass1[3]()
    z_handed(0)
    z_jump_far(1)
    near2()

    def add_up(k, carry):
        x = xg[k, :, :FEAT, :].astype(F32)
        return carry + jnp.sum(x.reshape(2 * FEAT, TOK), axis=0, keepdims=True)

    width = n_dev * 2 * FEAT
    centre = lax.fori_loop(0, n_dev, add_up, jnp.zeros((1, TOK), F32)) / width

    def add_square(k, carry):
        x = xg[k, :, :FEAT, :].astype(F32).reshape(2 * FEAT, TOK) - centre
        return carry + jnp.sum(x * x, axis=0, keepdims=True)

    spread = lax.fori_loop(0, n_dev, add_square, jnp.zeros((1, TOK), F32)) / width
    inverse = lax.rsqrt(spread + EPSILON)

    def modulate(k, carry):
        for j in (0, 1):
            x = (xg[k, j, :FEAT, :].astype(F32) - centre) * inverse
            wide = dot_tn(xg[k, j, FEAT:, :], pick)
            top = (x[:TOK] * (1.0 + wide[:, :TOK]) + wide[:, TOK : 2 * TOK]).astype(BF16)
            low = wide[: FEAT - TOK]
            rest = (x[TOK:] * (1.0 + low[:, 2 * TOK : 3 * TOK]) + low[:, 3 * TOK : 4 * TOK]).astype(
                BF16
            )
            top_mod = wide[:, 4 * TOK : 5 * TOK].astype(BF16)
            rest_mod = low[:, 5 * TOK :].astype(BF16)
            if j == 0:
                xm[k, 0:128, 0:TOK] = top
                xm[k, 128:160, 0:TOK] = rest
                xm[k, 0:128, TOK:] = top_mod
                xm[k, 128:160, TOK:] = rest_mod
            else:
                xm[k, 160:256, 0:TOK] = top[:96]
                xm[k, 320:352, 0:TOK] = top[96:]
                xm[k, 352:384, 0:TOK] = rest
                xm[k, 160:256, TOK:] = top_mod[:96]
                xm[k, 320:352, TOK:] = top_mod[96:]
                xm[k, 352:384, TOK:] = rest_mod
        return carry

    lax.fori_loop(0, n_dev // 2, modulate, 0)
    far2()
    z_near(1, 0)
    pass2[0]()
    lax.fori_loop(n_dev // 2, n_dev, modulate, 0)
    z_near(1, 1)
    z_near(1, 2)
    for act in end1:
        act()

    pre[...] = jnp.zeros((HID, 2 * TOK), F32)

    def first(k, carry):
        pre[...] += dot(w1[k], xm[k])
        return carry

    lax.fori_loop(0, n_dev // 2, first, 0)
    z_near(1, 3)
    pass2[1]()
    lax.fori_loop(n_dev // 2, n_dev, first, 0)
    pass2[2]()

    def tangent_of(v):
        return jnp.tanh(COEFF * (v + CUBIC * v * v * v))

    def split_store(ref, value):
        for start in range(0, HID, TOK):
            stop = min(start + TOK, HID)
            ref[:, start:stop] = value[start:stop].T.astype(BF16)

    v = pre[:, :TOK]
    split_store(act_t, 0.5 * v * (1.0 + tangent_of(v)))

    half_z = n_dev // 2

    class Sum:
        def __init__(self, i, part, hand, left, outl, right, outr):
            self.i = i
            self.part, self.hand = part, hand
            self.land, self.out = (left, right), (outl, outr)

        def owner(self, side_of, s):
            return wrap(z - half_z - 1 + s if side_of == 0 else z + half_z - s, n_dev)

        def hand_over(self, d):
            copy = pltpu.make_async_remote_copy(
                src_ref=self.part.at[d, 1 - core],
                dst_ref=self.hand.at[d],
                send_sem=h_send.at[self.i, d],
                recv_sem=h_recv.at[self.i, d],
                device_id=partner,
                device_id_type=MESH,
            )
            copy.start()
            pending.append(copy)

        def both_cores(self, d):
            arrive(self.hand, d, partner, h_send.at[self.i, d], h_recv.at[self.i, d])
            return self.part[d, core] + self.hand[d]

        def link(self, side_of, s):
            return pltpu.make_async_remote_copy(
                src_ref=self.out[side_of].at[s - 1],
                dst_ref=self.land[side_of].at[s - 1],
                send_sem=s_send.at[self.i, side_of, s - 1],
                recv_sem=s_recv.at[self.i, side_of, s - 1],
                device_id=(row, col_of(-1 if side_of == 0 else 1)),
                device_id_type=MESH,
            )

        def from_chain(self, side_of, s):
            self.link(side_of, s).wait_recv()
            return self.land[side_of][s - 1].astype(F32)

        def step(self, s):
            for side_of in (0, 1):
                if side_of == 1 and s == half_z:
                    continue
                total = self.both_cores(self.owner(side_of, s))
                if s > 1:
                    total = total + self.from_chain(side_of, s - 1)
                self.out[side_of][s - 1] = total.astype(SUM_TYPE)
                copy = self.link(side_of, s)
                copy.start()
                pending.append(copy)

        def last(self):
            total = self.both_cores(z)
            total = total + self.from_chain(0, half_z)
            return total + self.from_chain(1, half_z - 1)

    sum_a = Sum(0, part_a, hand_a, left_a, outl_a, right_a, outr_a)
    sum_b = Sum(1, part_b, hand_b, left_b, outl_b, right_b, outr_b)

    def forward_block(d):
        acted = act_t[...]
        main = dot(acted, w2[d]).T
        rest = dot(acted, w1[d, :, MAIN:]).T
        part_a[d, 0] = main[:FEAT]
        part_a[d, 1, : MAIN - FEAT] = main[FEAT:]
        part_a[d, 1, MAIN - FEAT :] = rest[:REM]
        sum_a.hand_over(d)

    def backward_block(d):
        both = dot(pg_t[...], w1[d])
        main = both[:, :MAIN].T
        rest = both[:, MAIN:].T
        part_b[d, 0, :FEAT] = main[:FEAT]
        part_b[d, 1, : MAIN - FEAT] = main[FEAT:]
        part_b[d, 1, MAIN - FEAT : FEAT] = rest[REM:]
        sum_b.hand_over(d)

    actg[...] = jnp.zeros((HID, TOK), F32)
    offsets = (0, -1, 1, 2)

    def second(group, ring):
        for half in (0, 1):
            rows = pl.ds(*HALVES[half])

            def step(t, carry):
                here = offsets[group]
                k = row_of(here, ring + t) if half == 0 else row_of(ring + t, here)
                actg[rows] += dot(w2[k, rows], zr[k, :MAIN]) + dot(
                    w1[k, rows, MAIN:], zr[k, MAIN:]
                )
                return carry

            lax.fori_loop(0, 3 if ring < 0 else 1, step, 0)

    def forward(group):
        for a in range(group + 1):
            for b in range(group + 1):
                if max(a, b) == group and a + b < 6:
                    forward_block(row_of(offsets[a], offsets[b]))

    def finish2(group):
        end2[group]()
        second(group, 2)

    z_handed(1)
    second(0, -1)
    second(1, -1)
    finish2(0)
    forward(0)
    pass2[3]()
    finish2(1)
    forward(1)
    second(2, -1)
    finish2(2)
    second(3, -1)
    forward(2)
    forward(3)
    finish2(3)

    v = pre[:, :TOK]
    tangent = tangent_of(v)
    slope = 0.5 * (1.0 + tangent) + 0.5 * v * (1.0 - tangent * tangent) * COEFF * (
        1.0 + 3.0 * CUBIC * v * v
    )
    grad = (actg[...] * slope).astype(BF16).astype(F32)
    split_store(pg_t, grad)

    extra = pre[:, TOK:]
    ones = extra[:, 4:5]
    scaled = ones + jnp.where(in_one, extra[:, 0:1], extra[:, 1:2])
    shifted = jnp.where(in_one, extra[:, 2:3], extra[:, 3:4])
    sums = jnp.concatenate(
        [
            jnp.sum(grad * scaled, axis=0, keepdims=True),
            jnp.sum(grad * (v - shifted), axis=0, keepdims=True),
            jnp.zeros((SUMS - 2, TOK), F32),
        ],
        axis=0,
    )

    def put_sums(k, carry):
        part_b[k, 0, FEAT:] = sums
        part_b[k, 1, FEAT:] = sums
        return carry

    lax.fori_loop(0, n_dev, put_sums, 0)

    def backward(s):
        if s <= half_z:
            backward_block(sum_b.owner(0, s))
            backward_block(sum_b.owner(1, s) if s < half_z else z)

    backward(1)
    forward_block(row_of(2, 2))
    sum_b.step(1)
    sum_a.step(1)
    backward(2)
    for s in range(2, half_z + 1):
        sum_b.step(s)
        sum_a.step(s)
        backward(s + 1)

    x = xg[z, core, :FEAT, :].astype(F32)
    normed = (x - centre) * inverse
    gate = local[0]
    g = local[1]
    mine = dot_tn(tile, pick[:, : 4 * TOK])
    scale_one = 1.0 + jnp.concatenate(
        [mine[:, :TOK], mine[: FEAT - TOK, 2 * TOK : 3 * TOK]], axis=0
    )
    lane_at = lax.broadcasted_iota(jnp.int32, (FEAT, TOK), 1)

    def put(lanes, index, value):
        a = jnp.sum(value * first_mask, axis=1, keepdims=True)
        b = jnp.sum(value * second_mask, axis=1, keepdims=True)
        lanes = jnp.where(lane_at == index, a, lanes)
        return jnp.where(lane_at == index + 1, b, lanes)

    total = sum_b.last()
    mod_grad = total[:FEAT]
    first_mean = total[FEAT : FEAT + 1] / width
    second_mean = total[FEAT + 1 : FEAT + 2] / width
    norm_grad = mod_grad * scale_one
    input_out[...] = (
        live * (g + inverse * (norm_grad - first_mean - normed * second_mean))
    ).astype(BF16)
    lanes = put(jnp.zeros((FEAT, TOK), F32), 0, mod_grad)
    lanes = put(lanes, 8, mod_grad * normed)

    projected = sum_a.last()
    block_out[...] = (live * (x + gate * projected)).astype(BF16)
    lanes = put(lanes, 16, projected * g)
    high, low = lanes[:TOK].T, lanes[TOK:].T
    for i in range(3):
        mod_out[i, :, :TOK] = high[8 * i : 8 * i + 2]
        mod_out[i, :, TOK:] = low[8 * i : 8 * i + 2]

    for copy in pending:
        copy.wait_send()


def body(hidden_states, clip_lengths, modulation, fc1_weight, fc2_weight, out_grad):
    depth = lax.axis_size("col") // 2
    side = 4
    vmem = pl.BlockSpec(memory_space=pltpu.VMEM)
    smem = pl.BlockSpec(memory_space=pltpu.SMEM)
    dma = pltpu.SemaphoreType.DMA
    block, grad, mods = pl.pallas_call(
        lambda *refs: kernel(depth, side, *refs),
        out_shape=(
            jax.ShapeDtypeStruct((FEAT, TOK), BF16),
            jax.ShapeDtypeStruct((FEAT, TOK), BF16),
            jax.ShapeDtypeStruct((3, 2, FEAT), F32),
        ),
        in_specs=[vmem, smem] + [vmem] * 4,
        out_specs=(vmem, vmem, vmem),
        scratch_shapes=[
            pltpu.VMEM((16, HID, WIDE), BF16),
            pltpu.VMEM((16, HID, MAIN), BF16),
            pltpu.VMEM((depth, 2, MSG, TOK), BF16),
            pltpu.VMEM((depth, WIDE, TOK), BF16),
            pltpu.VMEM((depth, WIDE, 2 * TOK), BF16),
            pltpu.VMEM((HID, 2 * TOK), F32),
            pltpu.VMEM((HID, TOK), F32),
            pltpu.VMEM((TOK, HID), BF16),
            pltpu.VMEM((TOK, HID), BF16),
            pltpu.VMEM((depth, 2, FEAT, TOK), F32),
            pltpu.VMEM((depth, FEAT, TOK), F32),
            pltpu.VMEM((depth, 2, FEAT + SUMS, TOK), F32),
            pltpu.VMEM((depth, FEAT + SUMS, TOK), F32),
            pltpu.VMEM((depth // 2, FEAT, TOK), SUM_TYPE),
            pltpu.VMEM((depth // 2, FEAT + SUMS, TOK), SUM_TYPE),
            pltpu.VMEM((depth // 2, FEAT, TOK), SUM_TYPE),
            pltpu.VMEM((depth // 2, FEAT + SUMS, TOK), SUM_TYPE),
            pltpu.VMEM((depth // 2, FEAT, TOK), SUM_TYPE),
            pltpu.VMEM((depth // 2, FEAT + SUMS, TOK), SUM_TYPE),
            pltpu.VMEM((depth // 2, FEAT, TOK), SUM_TYPE),
            pltpu.VMEM((depth // 2, FEAT + SUMS, TOK), SUM_TYPE),
            pltpu.VMEM((2, FEAT, TOK), F32),
            dma((2, 2, 5, 4)),
            dma((2, 2, 5, 4)),
            dma((2, 15)),
            dma((2, 15)),
            dma((2, depth)),
            dma((2, depth)),
            dma((2, depth)),
            dma((2, depth)),
            dma((2, 2, depth // 2)),
            dma((2, 2, depth // 2)),
        ],
        compiler_params=pltpu.CompilerParams(
            collective_id=0, has_side_effects=True, vmem_limit_bytes=60000 * 1024
        ),
    )(
        hidden_states.T,
        clip_lengths,
        modulation.transpose(1, 0, 2),
        fc1_weight,
        fc2_weight.T,
        out_grad.T,
    )
    return block.T, grad.T, mods.transpose(1, 0, 2)


def solution(mesh):
    return jax.shard_map(
        body,
        mesh=mesh,
        in_specs=(
            P("row", "col"),
            P("row", None),
            P("row", None, "col"),
            P("row", "col"),
            P("col", "row"),
            P("row", "col"),
        ),
        out_specs=(P("row", "col"), P("row", "col"), P("row", None, "col")),
        check_vma=False,
    )
```

```python
import jax
import jax.numpy as jnp
from jax import lax
from jax.experimental import pallas as pl
from jax.experimental.pallas import tpu as pltpu
from jax.sharding import PartitionSpec as P

EPSILON = 1e-06
COEFF = 0.7978845608028654
CUBIC = 0.044715
MESH = pl.DeviceIdType.MESH
F32 = jnp.float32
BF16 = jnp.bfloat16
SUM_TYPE = jnp.bfloat16

TOK = 128
FEAT = 160
HID = 432
ROWF = 320
MAIN = 256
REM = ROWF - MAIN
WIDE = MAIN + 2 * REM
QUARTERS = ((0, 112), (112, 112), (224, 112), (336, 96))
HALVES = ((0, 224), (224, 208))
MSG = FEAT + 16
SUMS = 16


def dot(a, b):
    return jnp.dot(a, b, preferred_element_type=F32)


def dot_tn(a, b):
    return lax.dot_general(a, b, (((0,), (0,)), ((), ())), preferred_element_type=F32)


def kernel(
    depth,
    side,
    hidden_in,
    lengths_in,
    mod_in,
    fc1_in,
    fc2_in,
    grad_in,
    block_out,
    input_out,
    mod_out,
    w1,
    w2,
    xg,
    zr,
    xm,
    pre,
    actg,
    act_t,
    pg_t,
    ahead,
    part_a,
    hand_a,
    part_b,
    hand_b,
    left_a,
    left_b,
    outl_a,
    outl_b,
    right_a,
    right_b,
    outr_a,
    outr_b,
    local,
    w_send,
    w_recv,
    z_send,
    z_recv,
    p_send,
    p_recv,
    h_send,
    h_recv,
    s_send,
    s_recv,
):
    n_dev = depth
    row = lax.axis_index("row")
    col = lax.axis_index("col")
    px, py = row // side, row % side
    z, core = col // 2, col % 2

    def wrap(value, size):
        return lax.rem(value + 2 * size, size)

    def row_of(dx, dy):
        return wrap(px + dx, side) * side + wrap(py + dy, side)

    def col_of(dz):
        return wrap(z + dz, n_dev) * 2 + core

    def at_row(dx, dy):
        return (row_of(dx, dy), col)

    way = 1 - 2 * core

    def at_col(dz):
        return (row, col_of(way * dz))

    partner = (row, z * 2 + (1 - core))
    neighbours = [
        at_row(1, 0),
        at_row(-1, 0),
        at_row(0, 1),
        at_row(0, -1),
        partner,
    ] + [at_col(step) for step in (1, -1, 2, -2, 4, -4)]

    barrier = pltpu.get_barrier_semaphore()
    for device in neighbours:
        pl.semaphore_signal(barrier, inc=1, device_id=device, device_id_type=MESH)

    def clear(k, carry):
        zr[k, ROWF:, :] = jnp.zeros((REM, TOK), BF16)
        xm[k, MAIN:ROWF, :] = jnp.zeros((REM, 2 * TOK), BF16)
        return carry

    def flip(value):
        return value.astype(F32).T

    def own_weights(start, size):
        at = pl.ds(start, size)
        for f in range(0, MAIN, TOK):
            w1[row, at, f : f + TOK] = flip(fc1_in[f : f + TOK, at]).astype(BF16)
            w2[row, at, f : f + TOK] = flip(fc2_in[f : f + TOK, at]).astype(BF16)
        both = jnp.concatenate([fc2_in[MAIN:, at], fc1_in[MAIN:, at]], axis=0)
        w1[row, at, MAIN:] = flip(both).astype(BF16)

    for start in range(0, HID, TOK):
        own_weights(start, min(TOK, HID - start))
    pl.semaphore_wait(barrier, len(neighbours))

    pending = []

    def send(ref, at, device, ssem, rsem):
        copy = pltpu.make_async_remote_copy(
            src_ref=ref.at[at],
            dst_ref=ref.at[at],
            send_sem=ssem,
            recv_sem=rsem,
            device_id=device,
            device_id_type=MESH,
        )
        copy.start()
        pending.append(copy)

    def arrive(ref, at, device, ssem, rsem):
        pltpu.make_async_remote_copy(
            src_ref=ref.at[at],
            dst_ref=ref.at[at],
            send_sem=ssem,
            recv_sem=rsem,
            device_id=device,
            device_id_type=MESH,
        ).wait_recv()

    class Ring:
        def __init__(self, weight, half, group, base, along):
            self.ref = (w1, w2)[weight]
            self.weight, self.half, self.group = weight, half, group
            self.base, self.along = base, along

        def slot(self, offset):
            dx, dy = self.base
            if self.along == 0:
                return row_of(dx + offset, dy)
            return row_of(dx, dy + offset)

        def peer(self, offset):
            return at_row(offset, 0) if self.along == 0 else at_row(0, offset)

        def sems(self, i):
            at = (self.weight, self.half, self.group, i)
            return w_send.at[at], w_recv.at[at]

        def rows(self, quarter):
            if quarter is None:
                return pl.ds(*HALVES[self.half])
            return pl.ds(*QUARTERS[2 * self.half + quarter])

        def move(self, fn, offset, quarter, to, i):
            fn(self.ref, (self.slot(offset), self.rows(quarter)), self.peer(to), *self.sems(i))

        def start(self):
            self.move(send, 0, None, 1, 0)
            self.move(send, 0, None, -1, 1)

        def middle(self, side_of):
            if side_of < 0:
                self.move(arrive, -1, None, -1, 0)
                self.move(send, -1, 0, 1, 2)
            else:
                self.move(arrive, 1, None, 1, 1)
                self.move(send, 1, 1, -1, 3)

        def end(self):
            self.move(arrive, 2, 0, -1, 2)
            self.move(arrive, 2, 1, 1, 3)

    def rings_of(weight):
        first, second = [], []
        for half in (0, 1):
            first.append(Ring(weight, half, 0, (0, 0), half))
            for i, offset in enumerate((0, -1, 1, 2)):
                base = (offset, 0) if half == 0 else (0, offset)
                second.append(Ring(weight, half, 1 + i, base, 1 - half))
        return first, second

    def weight_steps(weight):
        first, second = rings_of(weight)

        def begin():
            for ring in first:
                ring.start()
            second[0].start()
            second[4].start()

        def near():
            for half in (0, 1):
                first[half].middle(-1)
                second[4 * half + 1].start()
            for half in (0, 1):
                first[half].middle(1)
                second[4 * half + 2].start()

        def far():
            for half in (0, 1):
                first[half].end()
                second[4 * half + 3].start()

        def pass_on(i):
            def act():
                for half in (0, 1):
                    second[4 * half + i].middle(-1)
                    second[4 * half + i].middle(1)

            return act

        def finish(i):
            def act():
                for half in (0, 1):
                    second[4 * half + i].end()

            return act

        return begin, near, far, [pass_on(i) for i in range(4)], [finish(i) for i in range(4)]

    begin1, near1, far1, pass1, end1 = weight_steps(0)
    begin2, near2, far2, pass2, end2 = weight_steps(1)

    def message(m, dz, who):
        k = wrap(z + (way if who is core else -way) * dz, n_dev)
        if m == 0:
            return xg, (k, who)
        return zr, (k, pl.ds(pl.multiple_of(who * FEAT, FEAT), FEAT))

    def hand_over(m, dz, i):
        ref, at = message(m, dz, core)
        send(ref, at, partner, p_send.at[m, i], p_recv.at[m, i])

    near_by = (1, -1, 2)
    bases = (0, -4, 4, 8)

    def base(j):
        return bases[j]

    def spread(m, j):
        ref, at = message(m, base(j), core)
        for i, step in enumerate(near_by):
            n = 3 + 3 * j + i
            send(ref, at, at_col(step), z_send.at[m, n], z_recv.at[m, n])

    def z_begin(m):
        ref, at = message(m, 0, core)
        for n, step in ((0, 4), (1, -4)):
            send(ref, at, at_col(step), z_send.at[m, n], z_recv.at[m, n])
        spread(m, 0)
        hand_over(m, 0, 0)

    def z_jump(m):
        ref, at = message(m, -4, core)
        arrive(ref, at, at_col(-4), z_send.at[m, 0], z_recv.at[m, 0])
        send(ref, at, at_col(4), z_send.at[m, 2], z_recv.at[m, 2])
        spread(m, 1)
        hand_over(m, -4, 1)
        ref, at = message(m, 4, core)
        arrive(ref, at, at_col(4), z_send.at[m, 1], z_recv.at[m, 1])
        spread(m, 2)
        hand_over(m, 4, 2)

    def z_jump_far(m):
        ref, at = message(m, -8, core)
        arrive(ref, at, at_col(-4), z_send.at[m, 2], z_recv.at[m, 2])
        spread(m, 3)
        hand_over(m, 8, 3)

    def z_near(m, j):
        for i, step in enumerate(near_by):
            n = 3 + 3 * j + i
            ref, at = message(m, base(j) - step, core)
            arrive(ref, at, at_col(-step), z_send.at[m, n], z_recv.at[m, n])
            hand_over(m, base(j) - step, 4 + 3 * j + i)

    def z_handed(m):
        for j in range(4):
            for i in range(4):
                offset = base(j) - ((0,) + near_by)[i]
                n = j if i == 0 else 3 + 3 * j + i
                ref, at = message(m, offset, 1 - core)
                arrive(ref, at, partner, p_send.at[m, n], p_recv.at[m, n])

    begin1()

    lane = lax.broadcasted_iota(jnp.int32, (1, TOK), 1)
    end_one = lengths_in[0, 0]
    end_two = end_one + lengths_in[0, 1]
    ones_row = jnp.ones((1, TOK), F32)
    zero_row = jnp.zeros((1, TOK), F32)
    in_one = lane < end_one
    first_mask = jnp.where(in_one, ones_row, zero_row)
    live = jnp.where(lane < end_two, ones_row, zero_row)
    second_mask = live - first_mask

    xg[z, core, :FEAT, :] = hidden_in[...]
    mods = [mod_in[i].astype(F32) for i in range(3)]
    at_row8 = lax.broadcasted_iota(jnp.int32, (8, FEAT), 0)
    rows = jnp.where(at_row8 == 4, 1.0, jnp.zeros((8, FEAT), F32))
    for i, source in enumerate((1, 0)):
        rows = jnp.where(at_row8 == 2 * i, mods[source][0:1], rows)
        rows = jnp.where(at_row8 == 2 * i + 1, mods[source][1:2], rows)
    rows = jnp.where(at_row8 == 5, mods[2][0:1], rows)
    rows = jnp.where(at_row8 == 6, mods[2][1:2], rows)
    tail = lax.broadcasted_iota(jnp.int32, (FEAT, TOK), 0) - TOK
    shift_lanes = jnp.where(
        tail == lax.broadcasted_iota(jnp.int32, (FEAT, TOK), 1),
        jnp.ones((FEAT, TOK), F32),
        jnp.zeros((FEAT, TOK), F32),
    ).astype(BF16)
    tile = jnp.concatenate([rows[:, :TOK], dot(rows.astype(BF16), shift_lanes)], axis=0).astype(BF16)
    xg[z, core, FEAT:, :] = tile

    pick_row = lax.broadcasted_iota(jnp.int32, (16, TOK), 0)
    pick_lane = lax.broadcasted_iota(jnp.int32, (16, TOK), 1)
    pick_zero = jnp.zeros((16, TOK), F32)

    def picker(at):
        low = jnp.where(pick_row == at + 1, second_mask, pick_zero)
        return jnp.where(pick_row == at, first_mask, low)

    def lanes_of(base):
        inside = (pick_row - base == pick_lane) & (pick_lane < 8)
        return jnp.where(inside, 1.0, pick_zero)

    pick = jnp.concatenate(
        [picker(0), picker(2), picker(8), picker(10), lanes_of(0), lanes_of(8)], axis=1
    ).astype(BF16)
    pick_gate = jnp.concatenate([picker(5), picker(13)], axis=1).astype(BF16)
    gates = dot_tn(tile, pick_gate)
    gate_here = jnp.concatenate([gates[:, :TOK], gates[: FEAT - TOK, TOK:]], axis=0)
    g_here = grad_in[...].astype(F32)
    local[0] = gate_here
    local[1] = g_here
    zr[z, pl.ds(pl.multiple_of(core * FEAT, FEAT), FEAT), :] = (live * gate_here * g_here).astype(
        BF16
    )
    z_begin(0)
    z_begin(1)
    lax.fori_loop(0, n_dev, clear, 0)
    near1()
    z_jump(0)
    far1()
    begin2()
    pass1[0]()
    z_jump_far(0)
    z_near(0, 0)
    pass1[1]()
    z_near(0, 1)
    z_near(0, 2)
    z_jump(1)
    pass1[2]()
    z_near(0, 3)
    pass1[3]()
    z_handed(0)
    z_jump_far(1)
    near2()

    def add_up(k, carry):
        x = xg[k, :, :FEAT, :].astype(F32)
        return carry + jnp.sum(x.reshape(2 * FEAT, TOK), axis=0, keepdims=True)

    width = n_dev * 2 * FEAT
    centre = lax.fori_loop(0, n_dev, add_up, jnp.zeros((1, TOK), F32)) / width

    def add_square(k, carry):
        x = xg[k, :, :FEAT, :].astype(F32).reshape(2 * FEAT, TOK) - centre
        return carry + jnp.sum(x * x, axis=0, keepdims=True)

    spread = lax.fori_loop(0, n_dev, add_square, jnp.zeros((1, TOK), F32)) / width
    inverse = lax.rsqrt(spread + EPSILON)

    def modulate(k, carry):
        for j in (0, 1):
            x = (xg[k, j, :FEAT, :].astype(F32) - centre) * inverse
            wide = dot_tn(xg[k, j, FEAT:, :], pick)
            top = (x[:TOK] * (1.0 + wide[:, :TOK]) + wide[:, TOK : 2 * TOK]).astype(BF16)
            low = wide[: FEAT - TOK]
            rest = (x[TOK:] * (1.0 + low[:, 2 * TOK : 3 * TOK]) + low[:, 3 * TOK : 4 * TOK]).astype(
                BF16
            )
            top_mod = wide[:, 4 * TOK : 5 * TOK].astype(BF16)
            rest_mod = low[:, 5 * TOK :].astype(BF16)
            if j == 0:
                xm[k, 0:128, 0:TOK] = top
                xm[k, 128:160, 0:TOK] = rest
                xm[k, 0:128, TOK:] = top_mod
                xm[k, 128:160, TOK:] = rest_mod
            else:
                xm[k, 160:256, 0:TOK] = top[:96]
                xm[k, 320:352, 0:TOK] = top[96:]
                xm[k, 352:384, 0:TOK] = rest
                xm[k, 160:256, TOK:] = top_mod[:96]
                xm[k, 320:352, TOK:] = top_mod[96:]
                xm[k, 352:384, TOK:] = rest_mod
        return carry

    lax.fori_loop(0, n_dev // 2, modulate, 0)
    far2()
    z_near(1, 0)
    pass2[0]()
    lax.fori_loop(n_dev // 2, n_dev, modulate, 0)
    z_near(1, 1)
    z_near(1, 2)
    for act in end1:
        act()

    pre[...] = jnp.zeros((HID, 2 * TOK), F32)

    def first(k, carry):
        pre[...] += dot(w1[k], xm[k])
        return carry

    lax.fori_loop(0, n_dev // 2, first, 0)
    z_near(1, 3)
    pass2[1]()
    lax.fori_loop(n_dev // 2, n_dev, first, 0)
    pass2[2]()

    def split_store(ref, value):
        for start in range(0, HID, TOK):
            stop = min(start + TOK, HID)
            ref[:, start:stop] = value[start:stop].T.astype(BF16)

    v = pre[:, :TOK]
    tangent = jnp.tanh(COEFF * (v + CUBIC * v * v * v))
    split_store(act_t, 0.5 * v * (1.0 + tangent))
    ahead[0] = 0.5 * (1.0 + tangent) + 0.5 * v * (1.0 - tangent * tangent) * COEFF * (
        1.0 + 3.0 * CUBIC * v * v
    )
    extra = pre[:, TOK:]
    ahead[1] = extra[:, 4:5] + jnp.where(in_one, extra[:, 0:1], extra[:, 1:2])
    ahead[2] = v - jnp.where(in_one, extra[:, 2:3], extra[:, 3:4])

    half_z = n_dev // 2

    class Sum:
        def __init__(self, i, part, hand, left, outl, right, outr):
            self.i = i
            self.part, self.hand = part, hand
            self.land, self.out = (left, right), (outl, outr)

        def owner(self, side_of, s):
            return wrap(z - half_z - 1 + s if side_of == 0 else z + half_z - s, n_dev)

        def hand_over(self, d):
            copy = pltpu.make_async_remote_copy(
                src_ref=self.part.at[d, 1 - core],
                dst_ref=self.hand.at[d],
                send_sem=h_send.at[self.i, d],
                recv_sem=h_recv.at[self.i, d],
                device_id=partner,
                device_id_type=MESH,
            )
            copy.start()
            pending.append(copy)

        def both_cores(self, d):
            arrive(self.hand, d, partner, h_send.at[self.i, d], h_recv.at[self.i, d])
            return self.part[d, core] + self.hand[d]

        def link(self, side_of, s):
            return pltpu.make_async_remote_copy(
                src_ref=self.out[side_of].at[s - 1],
                dst_ref=self.land[side_of].at[s - 1],
                send_sem=s_send.at[self.i, side_of, s - 1],
                recv_sem=s_recv.at[self.i, side_of, s - 1],
                device_id=(row, col_of(-1 if side_of == 0 else 1)),
                device_id_type=MESH,
            )

        def from_chain(self, side_of, s):
            self.link(side_of, s).wait_recv()
            return self.land[side_of][s - 1].astype(F32)

        def step(self, s):
            for side_of in (0, 1):
                if side_of == 1 and s == half_z:
                    continue
                total = self.both_cores(self.owner(side_of, s))
                if s > 1:
                    total = total + self.from_chain(side_of, s - 1)
                self.out[side_of][s - 1] = total.astype(SUM_TYPE)
                copy = self.link(side_of, s)
                copy.start()
                pending.append(copy)

        def last(self):
            total = self.both_cores(z)
            total = total + self.from_chain(0, half_z)
            return total + self.from_chain(1, half_z - 1)

    sum_a = Sum(0, part_a, hand_a, left_a, outl_a, right_a, outr_a)
    sum_b = Sum(1, part_b, hand_b, left_b, outl_b, right_b, outr_b)

    def forward_block(d):
        acted = act_t[...]
        main = dot(acted, w2[d]).T
        rest = dot(acted, w1[d, :, MAIN:]).T
        part_a[d, 0] = main[:FEAT]
        part_a[d, 1, : MAIN - FEAT] = main[FEAT:]
        part_a[d, 1, MAIN - FEAT :] = rest[:REM]
        sum_a.hand_over(d)

    def backward_block(d):
        both = dot(pg_t[...], w1[d])
        main = both[:, :MAIN].T
        rest = both[:, MAIN:].T
        part_b[d, 0, :FEAT] = main[:FEAT]
        part_b[d, 1, : MAIN - FEAT] = main[FEAT:]
        part_b[d, 1, MAIN - FEAT : FEAT] = rest[REM:]
        sum_b.hand_over(d)

    actg[...] = jnp.zeros((HID, TOK), F32)
    offsets = (0, -1, 1, 2)

    def second(group, ring):
        for half in (0, 1):
            rows = pl.ds(*HALVES[half])

            def step(t, carry):
                here = offsets[group]
                k = row_of(here, ring + t) if half == 0 else row_of(ring + t, here)
                actg[rows] += dot(w2[k, rows], zr[k, :MAIN]) + dot(
                    w1[k, rows, MAIN:], zr[k, MAIN:]
                )
                return carry

            lax.fori_loop(0, 3 if ring < 0 else 1, step, 0)

    def forward(group):
        for a in range(group + 1):
            for b in range(group + 1):
                if max(a, b) == group and a + b < 6:
                    forward_block(row_of(offsets[a], offsets[b]))

    def finish2(group):
        end2[group]()
        second(group, 2)

    z_handed(1)
    second(0, -1)
    second(1, -1)
    finish2(0)
    forward(0)
    pass2[3]()
    finish2(1)
    forward(1)
    second(2, -1)
    finish2(2)
    second(3, -1)
    forward(2)
    forward(3)
    finish2(3)
    forward_block(row_of(2, 2))

    grad = (actg[...] * ahead[0]).astype(BF16).astype(F32)
    split_store(pg_t, grad)
    sums = jnp.concatenate(
        [
            jnp.sum(grad * ahead[1], axis=0, keepdims=True),
            jnp.sum(grad * ahead[2], axis=0, keepdims=True),
            jnp.zeros((SUMS - 2, TOK), F32),
        ],
        axis=0,
    )

    def put_sums(k, carry):
        part_b[k, 0, FEAT:] = sums
        part_b[k, 1, FEAT:] = sums
        return carry

    lax.fori_loop(0, n_dev, put_sums, 0)

    def backward(s):
        if s <= half_z:
            backward_block(sum_b.owner(0, s))
            backward_block(sum_b.owner(1, s) if s < half_z else z)

    backward(1)
    sum_a.step(1)
    sum_b.step(1)
    backward(2)
    for s in range(2, half_z + 1):
        sum_a.step(s)
        sum_b.step(s)
        backward(s + 1)

    x = xg[z, core, :FEAT, :].astype(F32)
    normed = (x - centre) * inverse
    gate = local[0]
    g = local[1]
    mine = dot_tn(tile, pick[:, : 4 * TOK])
    scale_one = 1.0 + jnp.concatenate(
        [mine[:, :TOK], mine[: FEAT - TOK, 2 * TOK : 3 * TOK]], axis=0
    )
    lane_at = lax.broadcasted_iota(jnp.int32, (FEAT, TOK), 1)

    def put(lanes, index, value):
        a = jnp.sum(value * first_mask, axis=1, keepdims=True)
        b = jnp.sum(value * second_mask, axis=1, keepdims=True)
        lanes = jnp.where(lane_at == index, a, lanes)
        return jnp.where(lane_at == index + 1, b, lanes)

    projected = sum_a.last()
    block_out[...] = (live * (x + gate * projected)).astype(BF16)
    lanes = put(jnp.zeros((FEAT, TOK), F32), 16, projected * g)

    total = sum_b.last()
    mod_grad = total[:FEAT]
    first_mean = total[FEAT : FEAT + 1] / width
    second_mean = total[FEAT + 1 : FEAT + 2] / width
    norm_grad = mod_grad * scale_one
    input_out[...] = (
        live * (g + inverse * (norm_grad - first_mean - normed * second_mean))
    ).astype(BF16)
    lanes = put(lanes, 0, mod_grad)
    lanes = put(lanes, 8, mod_grad * normed)
    high, low = lanes[:TOK].T, lanes[TOK:].T
    for i in range(3):
        mod_out[i, :, :TOK] = high[8 * i : 8 * i + 2]
        mod_out[i, :, TOK:] = low[8 * i : 8 * i + 2]

    for copy in pending:
        copy.wait_send()


def body(hidden_states, clip_lengths, modulation, fc1_weight, fc2_weight, out_grad):
    depth = lax.axis_size("col") // 2
    side = 4
    vmem = pl.BlockSpec(memory_space=pltpu.VMEM)
    smem = pl.BlockSpec(memory_space=pltpu.SMEM)
    dma = pltpu.SemaphoreType.DMA
    block, grad, mods = pl.pallas_call(
        lambda *refs: kernel(depth, side, *refs),
        out_shape=(
            jax.ShapeDtypeStruct((FEAT, TOK), BF16),
            jax.ShapeDtypeStruct((FEAT, TOK), BF16),
            jax.ShapeDtypeStruct((3, 2, FEAT), F32),
        ),
        in_specs=[vmem, smem] + [vmem] * 4,
        out_specs=(vmem, vmem, vmem),
        scratch_shapes=[
            pltpu.VMEM((16, HID, WIDE), BF16),
            pltpu.VMEM((16, HID, MAIN), BF16),
            pltpu.VMEM((depth, 2, MSG, TOK), BF16),
            pltpu.VMEM((depth, WIDE, TOK), BF16),
            pltpu.VMEM((depth, WIDE, 2 * TOK), BF16),
            pltpu.VMEM((HID, 2 * TOK), F32),
            pltpu.VMEM((HID, TOK), F32),
            pltpu.VMEM((TOK, HID), BF16),
            pltpu.VMEM((TOK, HID), BF16),
            pltpu.VMEM((3, HID, TOK), F32),
            pltpu.VMEM((depth, 2, FEAT, TOK), F32),
            pltpu.VMEM((depth, FEAT, TOK), F32),
            pltpu.VMEM((depth, 2, FEAT + SUMS, TOK), F32),
            pltpu.VMEM((depth, FEAT + SUMS, TOK), F32),
            pltpu.VMEM((depth // 2, FEAT, TOK), SUM_TYPE),
            pltpu.VMEM((depth // 2, FEAT + SUMS, TOK), SUM_TYPE),
            pltpu.VMEM((depth // 2, FEAT, TOK), SUM_TYPE),
            pltpu.VMEM((depth // 2, FEAT + SUMS, TOK), SUM_TYPE),
            pltpu.VMEM((depth // 2, FEAT, TOK), SUM_TYPE),
            pltpu.VMEM((depth // 2, FEAT + SUMS, TOK), SUM_TYPE),
            pltpu.VMEM((depth // 2, FEAT, TOK), SUM_TYPE),
            pltpu.VMEM((depth // 2, FEAT + SUMS, TOK), SUM_TYPE),
            pltpu.VMEM((2, FEAT, TOK), F32),
            dma((2, 2, 5, 4)),
            dma((2, 2, 5, 4)),
            dma((2, 15)),
            dma((2, 15)),
            dma((2, depth)),
            dma((2, depth)),
            dma((2, depth)),
            dma((2, depth)),
            dma((2, 2, depth // 2)),
            dma((2, 2, depth // 2)),
        ],
        compiler_params=pltpu.CompilerParams(
            collective_id=0, has_side_effects=True, vmem_limit_bytes=60000 * 1024
        ),
    )(
        hidden_states.T,
        clip_lengths,
        modulation.transpose(1, 0, 2),
        fc1_weight,
        fc2_weight.T,
        out_grad.T,
    )
    return block.T, grad.T, mods.transpose(1, 0, 2)


def solution(mesh):
    return jax.shard_map(
        body,
        mesh=mesh,
        in_specs=(
            P("row", "col"),
            P("row", None),
            P("row", None, "col"),
            P("row", "col"),
            P("col", "row"),
            P("row", "col"),
        ),
        out_specs=(P("row", "col"), P("row", "col"), P("row", None, "col")),
        check_vma=False,
    )
```
